128 devices in a mesh: row: 16 (over x, y_lo, core), col: 8 (over y_hi, z).
Axes of the slice: x: 4, y: 4 (y_hi: 2, y_lo: 2; y = y_hi * 2 + y_lo), z: 4, core: 2. Of those that a mesh axis runs over, the one named last changes fastest.
Arguments:
- radar_tiles: bfloat16 [1024, 512, 256], P('row', 'col'), may hold values from -6 to 6
- conv_scale: float32 [256], replicated, may hold values from 0.5 to 1.5
- conv_shift: float32 [256], replicated, may hold values from -3 to 3
- expand_weight: bfloat16 [256, 1024], replicated, may hold values from -0.375 to 0.375
- expand_bias: float32 [1024], replicated, may hold values from -3 to 3
- depth_kernel: float32 [3, 3, 1024], replicated, may hold values from -2 to 2
- depth_bias: float32 [1024], replicated, may hold values from -3 to 3
- project_weight: bfloat16 [1024, 256], replicated, may hold values from -0.1875 to 0.1875
- block_gains: float32 [2, 256], replicated, may hold values from 0.5 to 1.5
- block_entry: bfloat16 [256, 768], replicated, may hold values from -0.375 to 0.375
- block_leave: bfloat16 [256, 256], replicated, may hold values from -0.375 to 0.375
- block_offsets: float32 [8, 64, 64], replicated, may hold values from -6 to 6
- block_widen: bfloat16 [256, 1024], replicated, may hold values from -0.375 to 0.375
- block_shrink: bfloat16 [1024, 256], replicated, may hold values from -0.1875 to 0.1875
- grid_gains: float32 [2, 256], replicated, may hold values from 0.5 to 1.5
- grid_entry: bfloat16 [256, 768], replicated, may hold values from -0.375 to 0.375
- grid_leave: bfloat16 [256, 256], replicated, may hold values from -0.375 to 0.375
- grid_offsets: float32 [8, 64, 64], replicated, may hold values from -6 to 6
- grid_widen: bfloat16 [256, 1024], replicated, may hold values from -0.375 to 0.375
- grid_shrink: bfloat16 [1024, 256], replicated, may hold values from -0.1875 to 0.1875
Outputs:
- refined: bfloat16 [1024, 512, 256], P('row', 'col')
The draws below stay inside these ranges and needn't reach their ends.
All inputs are finite; a program needn't handle non-finite values.
Results may differ from the reference program's by a relative error of at most 0.015.
Values may be sent and summed in bfloat16 or wider, within the bound.
No kernel may reach another device: no remote copies, remote signals or barrier semaphores. Data moves between devices by JAX's collectives and lax.ppermute only.
A program may use at most 128 MiB of HBM per device.

```python
import math
import jax
import jax.numpy as jnp
from jax import lax

D = 256
HEADS = 8
WIN = 8
INNER = 1024
HEIGHT = 1024
BREADTH = 512
N_ROW = 16
N_COL = 8


def level_of(rng, extent, shards, low, top_value):
    def one(dim, shards_of):
        steps = jax.random.uniform(jax.random.fold_in(jax.random.fold_in(rng, 6), dim), (shards_of,), jnp.float32, low / len(shards), top_value / len(shards))
        return jnp.repeat(jnp.exp(steps), extent[dim] // shards_of).reshape((-1,) + (1,) * (len(extent) - dim - 1))

    level = one(*shards[0])
    for cut in shards[1:]:
        level = level * one(*cut)
    return level


def noise(stream_key, dims, deviation, bound, pieces=(), kind=jnp.bfloat16):
    values = deviation * jax.random.normal(stream_key, dims, jnp.float32)
    if pieces:
        values = values * level_of(stream_key, dims, pieces, -0.22, 0.18)
    return jnp.clip(values, -bound, bound).astype(kind)


def setup_inputs(seed: int = 0) -> dict:
    key_of = jax.random.split(jax.random.key(seed), 21)
    radar_tiles = noise(key_of[0], (HEIGHT, BREADTH, D), 1.0, 6.0, ((0, 16), (1, 8)))
    conv_scale = jnp.clip(jax.random.uniform(key_of[1], (D,), jnp.float32, 0.5, 1.5), 0.5, 1.5)
    conv_shift = noise(key_of[2], (D,), 0.5, 3.0, (), jnp.float32)
    expand_weight = noise(key_of[3], (D, INNER), D ** -0.5, 0.375)
    expand_bias = noise(key_of[4], (INNER,), 0.5, 3.0, (), jnp.float32)
    depth_kernel = noise(key_of[5], (3, 3, INNER), 9 ** -0.5, 2.0, (), jnp.float32)
    depth_bias = noise(key_of[6], (INNER,), 0.5, 3.0, (), jnp.float32)
    project_weight = noise(key_of[7], (INNER, D), INNER ** -0.5, 0.1875)
    block_gains = jnp.clip(jax.random.uniform(key_of[8], (2, D), jnp.float32, 0.5, 1.5), 0.5, 1.5)
    block_entry = noise(key_of[9], (D, 3 * D), D ** -0.5, 0.375)
    block_leave = noise(key_of[10], (D, D), D ** -0.5, 0.375)
    block_offsets = noise(key_of[11], (HEADS, WIN * WIN, WIN * WIN), 1.0, 6.0, (), jnp.float32)
    block_widen = noise(key_of[12], (D, INNER), D ** -0.5, 0.375)
    block_shrink = noise(key_of[13], (INNER, D), INNER ** -0.5, 0.1875)
    grid_gains = jnp.clip(jax.random.uniform(key_of[14], (2, D), jnp.float32, 0.5, 1.5), 0.5, 1.5)
    grid_entry = noise(key_of[15], (D, 3 * D), D ** -0.5, 0.375)
    grid_leave = noise(key_of[16], (D, D), D ** -0.5, 0.375)
    grid_offsets = noise(key_of[17], (HEADS, WIN * WIN, WIN * WIN), 1.0, 6.0, (), jnp.float32)
    grid_widen = noise(key_of[18], (D, INNER), D ** -0.5, 0.375)
    grid_shrink = noise(key_of[19], (INNER, D), INNER ** -0.5, 0.1875)
    return {"radar_tiles": radar_tiles, "conv_scale": conv_scale, "conv_shift": conv_shift, "expand_weight": expand_weight, "expand_bias": expand_bias, "depth_kernel": depth_kernel, "depth_bias": depth_bias, "project_weight": project_weight, "block_gains": block_gains, "block_entry": block_entry, "block_leave": block_leave, "block_offsets": block_offsets, "block_widen": block_widen, "block_shrink": block_shrink, "grid_gains": grid_gains, "grid_entry": grid_entry, "grid_leave": grid_leave, "grid_offsets": grid_offsets, "grid_widen": grid_widen, "grid_shrink": grid_shrink}


epsilon = 1e-05

def layer_norm(values, gain_row):
    center = values - lax.optimization_barrier(jnp.mean(values, axis=-1, keepdims=True))
    spread = lax.optimization_barrier(jnp.mean(center * center, axis=-1, keepdims=True))
    return center * lax.rsqrt(spread + epsilon) * gain_row

def attend(windows, norm_gains, entry_weight, leave_weight, offset_table, widen_weight, shrink_weight):
    win_count, positions, channels = windows.shape
    head_count = offset_table.shape[0]
    head_size = channels // head_count
    flattened = windows.reshape(-1, channels).astype(jnp.float32)
    lifted = layer_norm(flattened, norm_gains[0]).astype(jnp.bfloat16)
    projected = jnp.dot(lifted, entry_weight, preferred_element_type=jnp.float32).astype(jnp.bfloat16)
    projected = projected.reshape(win_count, positions, 3, head_count, head_size).astype(jnp.float32)
    query_rows = projected[:, :, 0]
    key_rows = projected[:, :, 1]
    value_rows = projected[:, :, 2]
    score_scale = 1.0 / math.sqrt(head_size)
    scores = jnp.einsum('nqhd,nkhd->nhqk', query_rows, key_rows) * score_scale + offset_table
    weights = jnp.exp(scores)
    weights = (weights / lax.optimization_barrier(jnp.sum(weights, axis=-1, keepdims=True))).astype(jnp.bfloat16)
    mixture = jnp.einsum('nhqk,nkhd->nqhd', weights.astype(jnp.float32), value_rows)
    mixture = mixture.astype(jnp.bfloat16).reshape(-1, channels)
    attended = (flattened + jnp.dot(mixture, leave_weight, preferred_element_type=jnp.float32)).astype(jnp.bfloat16)
    second = layer_norm(attended.astype(jnp.float32), norm_gains[1]).astype(jnp.bfloat16)
    hidden = jax.nn.gelu(jnp.dot(second, widen_weight, preferred_element_type=jnp.float32)).astype(jnp.bfloat16)
    result = attended.astype(jnp.float32) + jnp.dot(hidden, shrink_weight, preferred_element_type=jnp.float32)
    return result.astype(jnp.bfloat16).reshape(win_count, positions, channels)

def reference(radar_tiles, conv_scale, conv_shift, expand_weight, expand_bias, depth_kernel, depth_bias, project_weight, block_gains, block_entry, block_leave, block_offsets, block_widen, block_shrink, grid_gains, grid_entry, grid_leave, grid_offsets, grid_widen, grid_shrink):
    source = radar_tiles.astype(jnp.float32)
    normed = (source * conv_scale + conv_shift).astype(jnp.bfloat16)
    padded = jnp.pad(normed, ((1, 1), (1, 1), (0, 0)))
    inside = jnp.pad(jnp.ones((HEIGHT, BREADTH, 1), jnp.float32), ((1, 1), (1, 1), (0, 0)))

    def strip_work(strip_index):
        first_row = strip_index * WIN
        window_in = lax.dynamic_slice_in_dim(padded, first_row, WIN + 2, 0)
        window_mask = lax.dynamic_slice_in_dim(inside, first_row, WIN + 2, 0)
        lifted = jax.nn.gelu(jnp.dot(window_in.reshape(-1, D), expand_weight, preferred_element_type=jnp.float32) + expand_bias).astype(jnp.bfloat16)
        lifted = lifted.reshape(WIN + 2, BREADTH + 2, INNER) * window_mask.astype(jnp.bfloat16)
        summed = jnp.zeros((WIN, BREADTH, INNER), jnp.float32)
        for shift_row in range(3):
            for shift_col in range(3):
                summed = summed + lifted[shift_row:shift_row + WIN, shift_col:shift_col + BREADTH].astype(jnp.float32) * depth_kernel[shift_row, shift_col]
        activated = jax.nn.gelu(summed + depth_bias).astype(jnp.bfloat16)
        rows_in = lax.dynamic_slice_in_dim(source, first_row, WIN, 0)
        product = jnp.dot(activated.reshape(-1, INNER), project_weight, preferred_element_type=jnp.float32)
        return (rows_in + product.reshape(WIN, BREADTH, D)).astype(jnp.bfloat16)
    section_one = lax.map(strip_work, jnp.arange(HEIGHT // WIN, dtype=jnp.int32)).reshape(HEIGHT, BREADTH, D)
    blocks = section_one.reshape(HEIGHT // WIN, WIN, BREADTH // WIN, WIN, D).transpose(0, 2, 1, 3, 4)
    blocks = blocks.reshape(N_ROW * N_COL, -1, WIN * WIN, D)

    def block_work(window_group):
        return attend(window_group, block_gains, block_entry, block_leave, block_offsets, block_widen, block_shrink)
    attended_tiles = lax.map(block_work, blocks)
    section_two = attended_tiles.reshape(HEIGHT // WIN, BREADTH // WIN, WIN, WIN, D).transpose(0, 2, 1, 3, 4)
    section_two = section_two.reshape(HEIGHT, BREADTH, D)
    grid_sets = section_two.reshape(WIN, HEIGHT // WIN, WIN, BREADTH // WIN, D).transpose(1, 3, 0, 2, 4)
    grid_sets = grid_sets.reshape(N_ROW * N_COL, -1, WIN * WIN, D)

    def grid_work(window_group):
        return attend(window_group, grid_gains, grid_entry, grid_leave, grid_offsets, grid_widen, grid_shrink)
    spread = lax.map(grid_work, grid_sets)
    refined = spread.reshape(HEIGHT // WIN, BREADTH // WIN, WIN, WIN, D).transpose(2, 0, 3, 1, 4)
    return refined.reshape(HEIGHT, BREADTH, D)
```

```python
import functools
import math

import jax
import jax.numpy as jnp
from jax import lax
from jax.experimental import pallas as pl
from jax.experimental.pallas import tpu as pltpu
from jax.sharding import Mesh, PartitionSpec as P

WIN = 8
STRIP = 8
epsilon = 1e-05
F32 = jnp.float32
BF16 = jnp.bfloat16
GELU_A = math.sqrt(2.0 / math.pi)
GELU_B = GELU_A * 0.044715
LOG2E = math.log2(math.e)


def twice_gelu(v):
    return v + v * jnp.tanh(v * (GELU_A + GELU_B * (v * v)))


def dot(a, b):
    return jnp.dot(a, b, preferred_element_type=F32)


def load_halves(ref, where):
    return jnp.concatenate([ref[0, where, :], ref[1, where, :]], axis=-1)


def store_halves(ref, where, values):
    ref[0, where, :] = values[:, :128]
    ref[1, where, :] = values[:, 128:]


def layer_norm(values, values_bf16, averager, gain):
    mean = dot(values_bf16, averager)
    center = values - jnp.concatenate([mean, mean], axis=-1)
    spread = dot((center * center).astype(BF16), averager)
    scale = lax.rsqrt(spread + epsilon)
    return (center * jnp.concatenate([scale, scale], axis=-1) * gain).astype(BF16)


def prepare_offsets(table_ref, offs_scr):
    heads = table_ref.shape[0]
    for pair in range(heads // 2):
        two = jnp.concatenate([table_ref[2 * pair], table_ref[2 * pair + 1]], axis=-1)
        offs_scr[:, pair * 128 : (pair + 1) * 128] = two * LOG2E


def attend_rows(rows, gains_ref, entry_ref, leave_ref, widen_ref, shrink_ref, offs_scr, scr):
    qkv_scr, prob_scr, mix_scr, hid_scr = scr
    count, channels = rows.shape
    windows = count // 64
    averager = jnp.full((channels, 128), 1.0 / channels, BF16)
    normed = layer_norm(rows, rows.astype(BF16), averager, gains_ref[0:1, :])
    for part in range(3):
        cut = slice(part * channels, (part + 1) * channels)
        qkv_scr[:, cut] = dot(normed, entry_ref[:, cut]).astype(BF16)
    scale = LOG2E / math.sqrt(32.0)
    lane = lax.broadcasted_iota(jnp.int32, (64, 128), 1) // 32
    masks = [(lane == h).astype(F32).astype(BF16) for h in range(4)]
    key_head = lax.broadcasted_iota(jnp.int32, (256, 256), 0) // 64
    out_head = lax.broadcasted_iota(jnp.int32, (256, 256), 1) // 64
    adder = (key_head == out_head).astype(F32).astype(BF16)
    for w in range(windows):
        here = slice(w * 64, (w + 1) * 64)
        for g in range(2):
            part = slice(g * 128, (g + 1) * 128)
            keys = qkv_scr[here, channels + g * 128 : channels + (g + 1) * 128]
            wide = jnp.concatenate([keys * m for m in masks], axis=0)
            score = lax.dot_general(
                qkv_scr[here, part], wide, (((1,), (1,)), ((), ())), preferred_element_type=F32
            )
            wide_part = slice(g * 256, (g + 1) * 256)
            prob = jnp.exp2(score * scale + offs_scr[:, wide_part])
            prob_scr[here, wide_part] = prob
    for g in range(2):
        wide_part = slice(g * 256, (g + 1) * 256)
        prob = prob_scr[:, wide_part]
        total = dot(prob.astype(BF16), adder)
        weight = (prob / total).astype(BF16)
        for w in range(windows):
            here = slice(w * 64, (w + 1) * 64)
            start = 2 * channels + g * 128
            vals = qkv_scr[here, start : start + 128]
            wide = jnp.concatenate([vals * m for m in masks], axis=0)
            mix_scr[here, g * 128 : (g + 1) * 128] = dot(weight[here], wide).astype(BF16)
    attended_bf16 = (rows + dot(mix_scr[...], leave_ref[...])).astype(BF16)
    attended = attended_bf16.astype(F32)
    second = layer_norm(attended, attended_bf16, averager, gains_ref[1:2, :])
    inner = widen_ref.shape[1]
    for cut in range(0, inner, 256):
        hid_scr[:, cut : cut + 256] = twice_gelu(dot(second, widen_ref[:, cut : cut + 256])).astype(
            BF16
        )
    return attended + 0.5 * dot(hid_scr[...], shrink_ref[...])


def conv_block_kernel(
    flags_ref,
    x_ref,
    above_ref,
    below_ref,
    sides_ref,
    first_sides_ref,
    scale_ref,
    shift_ref,
    expand_ref,
    expand_bias_ref,
    depth_ref,
    depth_bias_ref,
    project_ref,
    gains_ref,
    entry_ref,
    leave_ref,
    offsets_ref,
    widen_ref,
    shrink_ref,
    out_ref,
    x_scr,
    wide_scr,
    norm_scr,
    exp_scr,
    act_scr,
    prod_scr,
    offs_scr,
    *attend_scr,
):
    step = pl.program_id(0)
    steps = pl.num_programs(0)
    strip_tokens = STRIP * 64
    inner = expand_ref.shape[1]
    blocks = inner // 256

    def expand(ext_rows, row_count, first_slot_row, left, right):
        tokens = row_count * 64
        cells = x_scr[pl.ds(pl.multiple_of(ext_rows * 64, 64), tokens), :].astype(F32)
        store_halves(wide_scr, slice(0, tokens), cells)
        per = row_count * 8
        for low in range(8):
            part = load_halves(wide_scr, pl.ds(low, per, stride=8))
            norm_scr[low * per : (low + 1) * per, :] = (
                part * scale_ref[...] + shift_ref[...]
            ).astype(BF16)
        side = jnp.concatenate([left, right], axis=0)
        norm_scr[8 * per : 8 * per + 16, :] = (side * scale_ref[...] + shift_ref[...]).astype(BF16)

        sub = lax.broadcasted_iota(jnp.int32, (8, 256), 0)

        def one(block, carry):
            cut = pl.ds(pl.multiple_of(block * 256, 256), 256)
            bias = expand_bias_ref[:, cut]
            cells = twice_gelu(
                dot(norm_scr[0 : 8 * per + 16, :], expand_ref[:, cut]) + bias
            )
            for low in range(8):
                exp_scr[low + 1, pl.ds(first_slot_row, row_count), :, cut] = cells[
                    low * per : (low + 1) * per
                ].reshape(row_count, 8, 256)
            for y in range(row_count):
                last = cells[7 * per + y * 8 : 7 * per + y * 8 + 8]
                first = cells[y * 8 : y * 8 + 8]
                at_left = cells[8 * per + y : 8 * per + y + 1] * flags_ref[2]
                at_right = cells[8 * per + 8 + y : 8 * per + 9 + y] * flags_ref[3]
                exp_scr[0, first_slot_row + y, :, cut] = jnp.where(
                    sub == 0, at_left, pltpu.roll(last, 1, 0)
                )
                exp_scr[9, first_slot_row + y, :, cut] = jnp.where(
                    sub == 7, at_right, pltpu.roll(first, 7, 0)
                )
            return carry

        lax.fori_loop(0, blocks, one, 0)

    @pl.when(step == 0)
    def _():
        body = x_ref.shape[0]
        x_scr[0:64, :] = above_ref[...]
        x_scr[64 : 64 + body, :] = x_ref[...]
        x_scr[64 + body : 128 + body, :] = below_ref[...]
        prepare_offsets(offsets_ref, offs_scr)
        expand(0, 2, 0, first_sides_ref[0], first_sides_ref[1])
        for slot in range(10):
            exp_scr[slot, 0] = exp_scr[slot, 0] * flags_ref[0]

    @pl.when(step > 0)
    def _():
        for slot in range(10):
            exp_scr[slot, 0:2] = exp_scr[slot, 8:10]

    expand(step * STRIP + 2, STRIP, 2, sides_ref[0], sides_ref[1])

    @pl.when(step == steps - 1)
    def _():
        for slot in range(10):
            exp_scr[slot, 9] = exp_scr[slot, 9] * flags_ref[1]

    def convolve(block, carry):
        cut = pl.ds(pl.multiple_of(block * 256, 256), 256)
        taps = [
            [jnp.broadcast_to(0.5 * depth_ref[3 * s + t : 3 * s + t + 1, cut], (8, 256)) for t in range(3)]
            for s in range(3)
        ]
        bias = jnp.broadcast_to(depth_bias_ref[:, cut], (8, 256))
        for low in range(8):
            total = jnp.broadcast_to(bias[None], (8, 8, 256))
            for s in range(3):
                for t in range(3):
                    total = total + exp_scr[low + t, s : s + 8, :, cut] * taps[s][t][None]
            act_scr[low * 64 : (low + 1) * 64, cut] = (
                twice_gelu(total).reshape(64, 256).astype(BF16)
            )
        return carry

    lax.fori_loop(0, blocks, convolve, 0)
    store_halves(prod_scr, slice(0, strip_tokens), dot(act_scr[...], project_ref[...]))
    pieces = []
    for w in range(8):
        for y in range(8):
            pieces.append(load_halves(prod_scr, pl.ds(y * 8 + w, 8, stride=64)))
    product = jnp.concatenate(pieces, axis=0)
    source = x_scr[pl.ds(pl.multiple_of((step * STRIP + 1) * 64, 64), strip_tokens), :].astype(F32)
    source = source.reshape(8, 8, 8, 256).swapaxes(0, 1).reshape(strip_tokens, 256)
    rows = (source + 0.5 * product).astype(BF16).astype(F32)
    done = attend_rows(
        rows, gains_ref, entry_ref, leave_ref, widen_ref, shrink_ref, offs_scr, attend_scr
    )
    done = done.reshape(8, 8, 8, 256).swapaxes(0, 1).reshape(strip_tokens, 256)
    out_ref[...] = done.astype(BF16)


def grid_kernel(
    x_ref,
    gains_ref,
    entry_ref,
    leave_ref,
    offsets_ref,
    widen_ref,
    shrink_ref,
    out_ref,
    in_scr,
    back_scr,
    offs_scr,
    *attend_scr,
):
    @pl.when(pl.program_id(0) == 0)
    def _():
        prepare_offsets(offsets_ref, offs_scr)

    store_halves(in_scr, slice(0, 512), x_ref[...].astype(F32).reshape(512, 256))
    rows = jnp.concatenate([load_halves(in_scr, pl.ds(w, 64, stride=8)) for w in range(8)], axis=0)
    done = attend_rows(
        rows, gains_ref, entry_ref, leave_ref, widen_ref, shrink_ref, offs_scr, attend_scr
    )
    for w in range(8):
        store_halves(back_scr, pl.ds(w, 64, stride=8), done[w * 64 : (w + 1) * 64])
    out_ref[...] = load_halves(back_scr, slice(0, 512)).reshape(64, 8, 256).astype(BF16)


def attend_scratch():
    return [
        pltpu.VMEM((64, 512), F32),
        pltpu.VMEM((512, 768), BF16),
        pltpu.VMEM((512, 512), F32),
        pltpu.VMEM((512, 256), BF16),
        pltpu.VMEM((512, 1024), BF16),
    ]


def whole(shape):
    return pl.BlockSpec(shape, lambda i: (0,) * len(shape))


def conv_block(flags, x, part, parts, above, below, sides, first_sides, weights):
    tokens, channels = x.shape
    body = tokens // parts
    steps = body // (STRIP * 64)
    return pl.pallas_call(
        conv_block_kernel,
        grid=(steps,),
        in_specs=[
            pl.BlockSpec(memory_space=pltpu.SMEM),
            pl.BlockSpec((body, channels), lambda i: (part, 0)),
            whole((64, channels)) if above.shape[0] == 64 else pl.BlockSpec((64, channels), lambda i: (part * (body // 64) - 1, 0)),
            whole((64, channels)) if below.shape[0] == 64 else pl.BlockSpec((64, channels), lambda i: ((part + 1) * (body // 64), 0)),
            pl.BlockSpec((2, 8, channels), lambda i: (0, i, 0)),
            whole((2, 8, channels)),
        ]
        + [whole(w.shape) for w in weights],
        out_specs=pl.BlockSpec((STRIP * 64, channels), lambda i: (i, 0)),
        out_shape=jax.ShapeDtypeStruct((body, channels), BF16),
        scratch_shapes=[
            pltpu.VMEM((body + 128, channels), BF16),
            pltpu.VMEM((2, 512, 128), F32),
            pltpu.VMEM((528, channels), BF16),
            pltpu.VMEM((10, 10, 8, 1024), F32),
            pltpu.VMEM((512, 1024), BF16),
            pltpu.VMEM((2, 512, 128), F32),
        ]
        + attend_scratch(),
        compiler_params=pltpu.CompilerParams(vmem_limit_bytes=56 << 20),
        cost_estimate=pl.CostEstimate(
            flops=body * 2600000, bytes_accessed=body * 1024 + 4000000, transcendentals=0
        ),
        name="conv_block",
    )(flags, x, above, below, sides, first_sides, *weights)


def grid_attend(x, weights):
    sources, count, channels = x.shape
    return pl.pallas_call(
        grid_kernel,
        grid=(count // 8,),
        in_specs=[pl.BlockSpec((sources, 8, channels), lambda i: (0, i, 0))]
        + [whole(w.shape) for w in weights],
        out_specs=pl.BlockSpec((sources, 8, channels), lambda i: (0, i, 0)),
        out_shape=jax.ShapeDtypeStruct(x.shape, BF16),
        scratch_shapes=[pltpu.VMEM((2, 512, 128), F32), pltpu.VMEM((2, 512, 128), F32)]
        + attend_scratch(),
        compiler_params=pltpu.CompilerParams(vmem_limit_bytes=56 << 20),
        cost_estimate=pl.CostEstimate(
            flops=sources * count * 1600000, bytes_accessed=sources * count * 1024 + 4000000, transcendentals=0
        ),
        name="grid_attend",
    )(x, *weights)


ROW = ("row_hi", "core")
GROUP = ("row_hi", "col")


def shards(
    radar_tiles,
    conv_scale,
    conv_shift,
    expand_weight,
    expand_bias,
    depth_kernel,
    depth_bias,
    project_weight,
    block_gains,
    block_entry,
    block_leave,
    block_offsets,
    block_widen,
    block_shrink,
    grid_gains,
    grid_entry,
    grid_leave,
    grid_offsets,
    grid_widen,
    grid_shrink,
    parts=2,
):
    rows_here, cols_here, channels = radar_tiles.shape
    row_count, col_count = lax.axis_size(ROW), lax.axis_size("col")
    row, col = lax.axis_index(ROW), lax.axis_index("col")

    def shifted(values, axis, count, step):
        pairs = [(i, i + step) for i in range(count) if 0 <= i + step < count]
        return lax.ppermute(values, axis, pairs)

    above = shifted(radar_tiles[-1:], ROW, row_count, 1)
    below = shifted(radar_tiles[:1], ROW, row_count, -1)
    edges = [
        jnp.concatenate([above[:, e], radar_tiles[:, e], below[:, e]], axis=0) for e in (-1, 0)
    ]
    left = shifted(edges[0], "col", col_count, 1)
    right = shifted(edges[1], "col", col_count, -1)
    sides = jnp.stack([left, right]).astype(F32)
    x = radar_tiles.reshape(rows_here * cols_here, channels)
    above = above.reshape(cols_here, channels)
    below = below.reshape(cols_here, channels)
    weights = (
        conv_scale.reshape(1, -1),
        conv_shift.reshape(1, -1),
        expand_weight,
        expand_bias.reshape(1, -1),
        depth_kernel.reshape(9, -1),
        depth_bias.reshape(1, -1),
        project_weight,
        block_gains,
        block_entry,
        block_leave,
        block_offsets,
        block_widen,
        block_shrink,
    )
    grid_weights = (grid_gains, grid_entry, grid_leave, grid_offsets, grid_widen, grid_shrink)
    group = row_count // 2 * col_count
    span = rows_here // parts
    outs = []
    for part in range(parts):
        start = part * span
        flags = jnp.stack(
            [
                jnp.where(row > 0, 1.0, 0.0) if part == 0 else jnp.float32(1.0),
                jnp.where(row < row_count - 1, 1.0, 0.0) if part == parts - 1 else jnp.float32(1.0),
                jnp.where(col > 0, 1.0, 0.0),
                jnp.where(col < col_count - 1, 1.0, 0.0),
            ]
        ).astype(F32)
        first = jnp.pad(sides[:, start : start + 2], ((0, 0), (0, 6), (0, 0)))
        mine = conv_block(
            flags,
            x,
            part,
            parts,
            above if part == 0 else x,
            below if part == parts - 1 else x,
            sides[:, start + 2 : start + 2 + span],
            first,
            weights,
        )
        outgoing = mine.reshape(group, -1, channels)
        outs.append(lax.all_to_all(outgoing, GROUP, split_axis=0, concat_axis=0, tiled=True))
    finished = []
    for arrived in outs:
        spread = grid_attend(arrived, grid_weights)
        finished.append(lax.all_to_all(spread, GROUP, split_axis=0, concat_axis=0, tiled=True))
    return jnp.concatenate(
        [f.reshape(span, cols_here, channels) for f in finished], axis=0
    )


def solution(mesh):
    inner = Mesh(mesh.devices.reshape(8, 2, 8), ("row_hi", "core", "col"))
    tiles = P(ROW, "col", None)
    return jax.shard_map(
        shards,
        mesh=inner,
        in_specs=(tiles,) + (P(),) * 19,
        out_specs=tiles,
        check_vma=False,
    )
```

```python
import functools
import math

import jax
import jax.numpy as jnp
from jax import lax
from jax.experimental import pallas as pl
from jax.experimental.pallas import tpu as pltpu
from jax.sharding import Mesh, PartitionSpec as P

WIN = 8
STRIP = 16
GRID_WINDOWS = 16
epsilon = 1e-05
F32 = jnp.float32
BF16 = jnp.bfloat16
GELU_A = math.sqrt(2.0 / math.pi)
GELU_B = GELU_A * 0.044715
LOG2E = math.log2(math.e)


def twice_gelu(v):
    return v + v * jnp.tanh(v * (GELU_A + GELU_B * (v * v)))


def dot(a, b):
    return jnp.dot(a, b, preferred_element_type=F32)


def load_halves(ref, where):
    return jnp.concatenate([ref[0, where, :], ref[1, where, :]], axis=-1)


def store_halves(ref, where, values):
    ref[0, where, :] = values[:, :128]
    ref[1, where, :] = values[:, 128:]


def layer_norm(values, gain):
    mean = jnp.mean(values, axis=-1, keepdims=True)
    center = values - mean
    spread = jnp.mean(center * center, axis=-1, keepdims=True)
    return (center * lax.rsqrt(spread + epsilon) * gain).astype(BF16)


def halves_dot(a, b):
    half = a.shape[0] // 2
    return jnp.concatenate([dot(a[:half], b), dot(a[half:], b)], axis=0)


def prepare_offsets(table_ref, offs_scr):
    heads = table_ref.shape[0]
    for pair in range(heads // 2):
        two = jnp.concatenate([table_ref[2 * pair], table_ref[2 * pair + 1]], axis=-1)
        offs_scr[:, pair * 128 : (pair + 1) * 128] = two * LOG2E


def attend_rows(rows, gains_ref, entry_ref, leave_ref, widen_ref, shrink_ref, offs_scr):
    count, channels = rows.shape
    windows = count // 64
    normed = layer_norm(rows, gains_ref[0:1, :])
    scale = LOG2E / math.sqrt(32.0)
    qkv = [
        halves_dot(normed, entry_ref[:, part * channels : (part + 1) * channels])
        for part in range(3)
    ]
    queries = (qkv[0] * scale).astype(BF16)
    keys = qkv[1].astype(BF16)
    values = qkv[2].astype(BF16)
    lane = lax.broadcasted_iota(jnp.int32, (64, 128), 1) // 32
    masks = [(lane == h).astype(F32).astype(BF16) for h in range(4)]
    key_head = lax.broadcasted_iota(jnp.int32, (256, 256), 0) // 64
    out_head = lax.broadcasted_iota(jnp.int32, (256, 256), 1) // 64
    adder = (key_head == out_head).astype(F32).astype(BF16)
    sides = []
    for g in range(2):
        part = slice(g * 128, (g + 1) * 128)
        wide_part = slice(g * 256, (g + 1) * 256)
        probs = []
        for w in range(windows):
            here = slice(w * 64, (w + 1) * 64)
            wide = jnp.concatenate([keys[here, part] * m for m in masks], axis=0)
            score = lax.dot_general(
                queries[here, part], wide, (((1,), (1,)), ((), ())), preferred_element_type=F32
            )
            probs.append(jnp.exp2(score + offs_scr[:, wide_part]))
        prob = jnp.concatenate(probs, axis=0)
        total = halves_dot(prob.astype(BF16), adder)
        weight = (prob / total).astype(BF16)
        mixed = []
        for w in range(windows):
            here = slice(w * 64, (w + 1) * 64)
            wide = jnp.concatenate([values[here, part] * m for m in masks], axis=0)
            mixed.append(dot(weight[here], wide).astype(BF16))
        sides.append(jnp.concatenate(mixed, axis=0))
    mixture = jnp.concatenate(sides, axis=-1)
    attended = (rows + halves_dot(mixture, leave_ref[...])).astype(BF16).astype(F32)
    second = layer_norm(attended, gains_ref[1:2, :])
    inner = widen_ref.shape[1]
    hidden = jnp.concatenate(
        [
            twice_gelu(halves_dot(second, widen_ref[:, cut : cut + 256]).astype(BF16))
            for cut in range(0, inner, 256)
        ],
        axis=-1,
    )
    return attended + 0.5 * halves_dot(hidden, shrink_ref[...])


def conv_block_kernel(
    flags_ref,
    x_ref,
    above_ref,
    below_ref,
    sides_ref,
    scale_ref,
    shift_ref,
    expand_ref,
    expand_bias_ref,
    depth_ref,
    depth_bias_ref,
    project_ref,
    gains_ref,
    entry_ref,
    leave_ref,
    offsets_ref,
    widen_ref,
    shrink_ref,
    out_ref,
    x_scr,
    wide_scr,
    prod_scr,
    offs_scr,
):
    step = pl.program_id(0)
    steps = pl.num_programs(0)
    tokens = STRIP * 64
    inner = expand_ref.shape[1]

    @pl.when(step == 0)
    def _():
        body = x_ref.shape[0]
        x_scr[0:64, :] = above_ref[...]
        x_scr[64 : 64 + body, :] = x_ref[...]
        x_scr[64 + body : 128 + body, :] = below_ref[...]
        prepare_offsets(offsets_ref, offs_scr)

    ext = STRIP + 2
    start = pl.multiple_of(step * tokens, tokens)
    store_halves(
        wide_scr, slice(0, ext * 64), x_scr[pl.ds(start, ext * 64), :].astype(F32)
    )
    where_in = lax.broadcasted_iota(jnp.int32, (ext, 8, 256), 1)
    scale = scale_ref[...][None]
    shift = shift_ref[...][None]

    def paired(cells):
        both = jnp.stack([cells[:10], cells[8:18]], axis=1)
        return (both * scale[None] + shift[None]).reshape(160, 256).astype(BF16)

    def side(which):
        rows = sides_ref[which, pl.ds(pl.multiple_of(step * STRIP, 8), 24), :]
        return jnp.broadcast_to(rows[:ext, None, :], (ext, 8, 256))

    slots = [None] * 10
    for low in range(8):
        cells = load_halves(wide_scr, pl.ds(low, ext * 8, stride=8))
        slots[low + 1] = paired(cells.reshape(ext, 8, 256))
        if low == 7:
            rolled = pltpu.roll(cells, 1, 0).reshape(ext, 8, 256)
            slots[0] = paired(jnp.where(where_in == 0, side(0), rolled))
        if low == 0:
            rolled = pltpu.roll(cells, ext * 8 - 1, 0).reshape(ext, 8, 256)
            slots[9] = paired(jnp.where(where_in == 7, side(1), rolled))

    sub = lax.broadcasted_iota(jnp.int32, (16, 256), 0)

    def keep(condition, flag):
        return jnp.where(condition, flag, 1.0).astype(BF16)

    top = keep(sub < 8, jnp.where(step == 0, flags_ref[0], 1.0))
    bottom = keep(sub >= 8, jnp.where(step == steps - 1, flags_ref[1], 1.0))
    at_left = keep(sub % 8 == 0, flags_ref[2])
    at_right = keep(sub % 8 == 7, flags_ref[3])

    product = [None] * 8
    for cut in range(0, inner, 256):
        here = slice(cut, cut + 256)
        bias = expand_bias_ref[:, here]
        cells = []
        for slot in range(10):
            one = twice_gelu((dot(slots[slot], expand_ref[:, here]) + bias).astype(BF16))
            one = one.reshape(10, 16, 256)
            one = jnp.concatenate([one[:1] * top[None], one[1:9], one[9:] * bottom[None]], axis=0)
            if slot == 0:
                one = one * at_left[None]
            if slot == 9:
                one = one * at_right[None]
            cells.append(one)
        taps = (0.5 * depth_ref[:, here]).astype(BF16)
        depth_bias = depth_bias_ref[:, here].astype(BF16)
        for low in range(8):
            total = depth_bias[None]
            for s in range(3):
                for t in range(3):
                    tap = taps[3 * s + t : 3 * s + t + 1][None]
                    total = total + cells[low + t][s : s + 8] * tap
            part = dot(twice_gelu(total).reshape(128, 256), project_ref[here, :])
            product[low] = part if product[low] is None else product[low] + part
    for low in range(8):
        store_halves(prod_scr, slice(low * 128, (low + 1) * 128), product[low])
    pieces = []
    for w in range(16):
        for y in range(8):
            pieces.append(load_halves(prod_scr, pl.ds(y * 16 + w, 8, stride=128)))
    source = x_scr[pl.ds(pl.multiple_of(start + 64, 64), tokens), :].astype(F32)
    source = source.reshape(2, 8, 8, 8, 256).swapaxes(1, 2).reshape(tokens, 256)
    rows = (source + 0.5 * jnp.concatenate(pieces, axis=0)).astype(BF16).astype(F32)
    done = attend_rows(
        rows, gains_ref, entry_ref, leave_ref, widen_ref, shrink_ref, offs_scr
    )
    done = done.reshape(2, 8, 8, 8, 256).swapaxes(1, 2).reshape(tokens, 256)
    out_ref[...] = done.astype(BF16)


def grid_kernel(
    x_ref,
    gains_ref,
    entry_ref,
    leave_ref,
    offsets_ref,
    widen_ref,
    shrink_ref,
    out_ref,
    in_scr,
    back_scr,
    offs_scr,
):
    @pl.when(pl.program_id(0) == 0)
    def _():
        prepare_offsets(offsets_ref, offs_scr)

    count = x_ref.shape[1]
    tokens = count * 64
    store_halves(in_scr, slice(0, tokens), x_ref[...].astype(F32).reshape(tokens, 256))
    rows = jnp.concatenate(
        [load_halves(in_scr, pl.ds(w, 64, stride=count)) for w in range(count)], axis=0
    )
    done = attend_rows(
        rows, gains_ref, entry_ref, leave_ref, widen_ref, shrink_ref, offs_scr
    )
    for w in range(count):
        store_halves(back_scr, pl.ds(w, 64, stride=count), done[w * 64 : (w + 1) * 64])
    out_ref[...] = load_halves(back_scr, slice(0, tokens)).reshape(64, count, 256).astype(BF16)


def attend_scratch():
    return [pltpu.VMEM((64, 512), F32)]


def whole(shape):
    return pl.BlockSpec(shape, lambda i: (0,) * len(shape))


def conv_block(flags, x, part, parts, above, below, sides, weights):
    tokens, channels = x.shape
    body = tokens // parts
    steps = body // (STRIP * 64)

    def border(rows, index):
        if rows.shape[0] == 64:
            return whole((64, channels))
        return pl.BlockSpec((64, channels), lambda i: (index, 0))

    return pl.pallas_call(
        conv_block_kernel,
        grid=(steps,),
        in_specs=[
            pl.BlockSpec(memory_space=pltpu.SMEM),
            pl.BlockSpec((body, channels), lambda i: (part, 0)),
            border(above, part * (body // 64) - 1),
            border(below, (part + 1) * (body // 64)),
            whole(sides.shape),
        ]
        + [whole(w.shape) for w in weights],
        out_specs=pl.BlockSpec((STRIP * 64, channels), lambda i: (i, 0)),
        out_shape=jax.ShapeDtypeStruct((body, channels), BF16),
        scratch_shapes=[
            pltpu.VMEM((body + 128, channels), BF16),
            pltpu.VMEM((2, (STRIP + 2) * 64, 128), F32),
            pltpu.VMEM((2, STRIP * 64, 128), F32),
            pltpu.VMEM((64, 512), F32),
        ],
        compiler_params=pltpu.CompilerParams(vmem_limit_bytes=56 << 20),
        cost_estimate=pl.CostEstimate(
            flops=body * 2600000, bytes_accessed=body * 1024 + 4000000, transcendentals=0
        ),
        name="conv_block",
    )(flags, x, above, below, sides, *weights)


def grid_attend(x, weights):
    sources, count, channels = x.shape
    block = pl.BlockSpec((sources, GRID_WINDOWS, channels), lambda i: (0, i, 0))
    tokens = sources * GRID_WINDOWS
    return pl.pallas_call(
        grid_kernel,
        grid=(count // GRID_WINDOWS,),
        in_specs=[block] + [whole(w.shape) for w in weights],
        out_specs=block,
        out_shape=jax.ShapeDtypeStruct(x.shape, BF16),
        scratch_shapes=[
            pltpu.VMEM((2, tokens, 128), F32),
            pltpu.VMEM((2, tokens, 128), F32),
            pltpu.VMEM((64, 512), F32),
        ],
        compiler_params=pltpu.CompilerParams(vmem_limit_bytes=56 << 20),
        cost_estimate=pl.CostEstimate(
            flops=sources * count * 1600000,
            bytes_accessed=sources * count * 1024 + 4000000,
            transcendentals=0,
        ),
        name="grid_attend",
    )(x, *weights)


ROW = ("row_hi", "core")
GROUP = ("row_hi", "col")


def shards(
    radar_tiles,
    conv_scale,
    conv_shift,
    expand_weight,
    expand_bias,
    depth_kernel,
    depth_bias,
    project_weight,
    block_gains,
    block_entry,
    block_leave,
    block_offsets,
    block_widen,
    block_shrink,
    grid_gains,
    grid_entry,
    grid_leave,
    grid_offsets,
    grid_widen,
    grid_shrink,
    parts=2,
):
    rows_here, cols_here, channels = radar_tiles.shape
    row_count, col_count = lax.axis_size(ROW), lax.axis_size("col")
    row, col = lax.axis_index(ROW), lax.axis_index("col")

    def shifted(values, axis, count, step):
        pairs = [(i, i + step) for i in range(count) if 0 <= i + step < count]
        return lax.ppermute(values, axis, pairs)

    above = shifted(radar_tiles[-1:], ROW, row_count, 1)
    below = shifted(radar_tiles[:1], ROW, row_count, -1)
    edges = [
        jnp.concatenate([above[:, e], radar_tiles[:, e], below[:, e]], axis=0) for e in (-1, 0)
    ]
    left = shifted(edges[0], "col", col_count, 1)
    right = shifted(edges[1], "col", col_count, -1)
    sides = jnp.stack([left, right]).astype(F32)
    x = radar_tiles.reshape(rows_here * cols_here, channels)
    above = above.reshape(cols_here, channels)
    below = below.reshape(cols_here, channels)
    weights = (
        conv_scale.reshape(1, -1),
        conv_shift.reshape(1, -1),
        expand_weight,
        expand_bias.reshape(1, -1),
        depth_kernel.reshape(9, -1),
        depth_bias.reshape(1, -1),
        project_weight,
        block_gains,
        block_entry,
        block_leave,
        block_offsets,
        block_widen,
        block_shrink,
    )
    grid_weights = (grid_gains, grid_entry, grid_leave, grid_offsets, grid_widen, grid_shrink)
    group = row_count // 2 * col_count
    span = rows_here // parts
    outs = []
    for part in range(parts):
        start = part * span
        flags = jnp.stack(
            [
                jnp.where(row > 0, 1.0, 0.0) if part == 0 else jnp.float32(1.0),
                jnp.where(row < row_count - 1, 1.0, 0.0) if part == parts - 1 else jnp.float32(1.0),
                jnp.where(col > 0, 1.0, 0.0),
                jnp.where(col < col_count - 1, 1.0, 0.0),
            ]
        ).astype(F32)
        mine = conv_block(
            flags,
            x,
            part,
            parts,
            above if part == 0 else x,
            below if part == parts - 1 else x,
            jnp.pad(sides[:, start : start + span + 2], ((0, 0), (0, 6), (0, 0))),
            weights,
        )
        outgoing = mine.reshape(group, -1, channels)
        outs.append(lax.all_to_all(outgoing, GROUP, split_axis=0, concat_axis=0, tiled=True))
    finished = []
    for arrived in outs:
        spread = grid_attend(arrived, grid_weights)
        finished.append(lax.all_to_all(spread, GROUP, split_axis=0, concat_axis=0, tiled=True))
    return jnp.concatenate(
        [f.reshape(span, cols_here, channels) for f in finished], axis=0
    )


def solution(mesh):
    inner = Mesh(mesh.devices.reshape(8, 2, 8), ("row_hi", "core", "col"))
    tiles = P(ROW, "col", None)
    return jax.shard_map(
        shards,
        mesh=inner,
        in_specs=(tiles,) + (P(),) * 19,
        out_specs=tiles,
        check_vma=False,
    )
```

```python
import functools
import math

import jax
import jax.numpy as jnp
from jax import lax
from jax.experimental import pallas as pl
from jax.experimental.pallas import tpu as pltpu
from jax.sharding import Mesh, PartitionSpec as P

WIN = 8
STRIP = 16
GRID_WINDOWS = 16
epsilon = 1e-05
F32 = jnp.float32
BF16 = jnp.bfloat16
GELU_A = math.sqrt(2.0 / math.pi)
GELU_B = GELU_A * 0.044715
LOG2E = math.log2(math.e)


GELU_S = GELU_B ** (1.0 / 3.0)
GELU_C = GELU_A / GELU_S
GELU_BACK = 0.5 / GELU_S


def scaled_gelu(z):
    return z + z * jnp.tanh(z * (z * z + GELU_C))


def dot(a, b):
    return jnp.dot(a, b, preferred_element_type=F32)


def load_halves(ref, where):
    return jnp.concatenate([ref[0, where, :], ref[1, where, :]], axis=-1)


def store_halves(ref, where, values):
    ref[0, where, :] = values[:, :128]
    ref[1, where, :] = values[:, 128:]


def layer_norm(values, gain):
    mean = jnp.mean(values, axis=-1, keepdims=True)
    center = values - mean
    spread = jnp.mean(center * center, axis=-1, keepdims=True)
    return (center * lax.rsqrt(spread + epsilon) * gain).astype(BF16)


def halves_dot(a, b):
    half = a.shape[0] // 2
    return jnp.concatenate([dot(a[:half], b), dot(a[half:], b)], axis=0)


def prepare_offsets(table_ref, offs_scr):
    heads = table_ref.shape[0]
    for pair in range(heads // 2):
        two = jnp.concatenate([table_ref[2 * pair], table_ref[2 * pair + 1]], axis=-1)
        offs_scr[:, pair * 128 : (pair + 1) * 128] = two * LOG2E


def attend_rows(rows, gains_ref, entry_ref, leave_ref, widen_ref, shrink_ref, offs_scr):
    count, channels = rows.shape
    windows = count // 64
    normed = layer_norm(rows, gains_ref[0:1, :])
    scale = LOG2E / math.sqrt(32.0)
    qkv = [
        halves_dot(normed, entry_ref[:, part * channels : (part + 1) * channels])
        for part in range(3)
    ]
    queries = (qkv[0] * scale).astype(BF16)
    keys = qkv[1].astype(BF16)
    values = qkv[2].astype(BF16)
    lane = lax.broadcasted_iota(jnp.int32, (64, 128), 1) // 32
    masks = [(lane == h).astype(F32).astype(BF16) for h in range(4)]
    key_head = lax.broadcasted_iota(jnp.int32, (256, 256), 0) // 64
    out_head = lax.broadcasted_iota(jnp.int32, (256, 256), 1) // 64
    adder = (key_head == out_head).astype(F32).astype(BF16)
    sides = []
    for g in range(2):
        part = slice(g * 128, (g + 1) * 128)
        wide_part = slice(g * 256, (g + 1) * 256)
        probs = []
        for w in range(windows):
            here = slice(w * 64, (w + 1) * 64)
            wide = jnp.concatenate([keys[here, part] * m for m in masks], axis=0)
            score = lax.dot_general(
                queries[here, part], wide, (((1,), (1,)), ((), ())), preferred_element_type=F32
            )
            probs.append(jnp.exp2(score + offs_scr[:, wide_part]))
        prob = jnp.concatenate(probs, axis=0)
        total = halves_dot(prob.astype(BF16), adder)
        weight = (prob / total).astype(BF16)
        mixed = []
        for w in range(windows):
            here = slice(w * 64, (w + 1) * 64)
            wide = jnp.concatenate([values[here, part] * m for m in masks], axis=0)
            mixed.append(dot(weight[here], wide).astype(BF16))
        sides.append(jnp.concatenate(mixed, axis=0))
    mixture = jnp.concatenate(sides, axis=-1)
    attended = (rows + halves_dot(mixture, leave_ref[...])).astype(BF16).astype(F32)
    second = layer_norm(attended, GELU_S * gains_ref[1:2, :])
    inner = widen_ref.shape[1]
    hidden = jnp.concatenate(
        [
            scaled_gelu(halves_dot(second, widen_ref[:, cut : cut + 256]).astype(BF16))
            for cut in range(0, inner, 256)
        ],
        axis=-1,
    )
    return attended + GELU_BACK * halves_dot(hidden, shrink_ref[...])


def conv_block_kernel(edge, x_ref, above_ref, below_ref, *refs):
    if edge:
        halo_above_ref, halo_below_ref = refs[:2]
        refs = refs[2:]
    (
        left_ref,
        right_ref,
        scale_ref,
        shift_ref,
        expand_ref,
        expand_bias_ref,
        depth_ref,
        depth_bias_ref,
        project_ref,
        gains_ref,
        entry_ref,
        leave_ref,
        offsets_ref,
        widen_ref,
        shrink_ref,
        out_ref,
        wide_scr,
        side_scr,
        prod_scr,
        offs_scr,
    ) = refs
    step = pl.program_id(0)
    steps = pl.num_programs(0)
    tokens = STRIP * 64
    inner = expand_ref.shape[1]

    @pl.when(step == 0)
    def _():
        prepare_offsets(offsets_ref, offs_scr)
        for which, ref in enumerate((left_ref, right_ref)):
            side = ref[...].astype(F32)
            first = 0 if edge else STRIP
            second = side.shape[0] - STRIP - 2 - first
            side_scr[which, 0:18, :] = side[first : first + 18]
            side_scr[which, 24:42, :] = side[second : second + 18]

    above = above_ref[...].astype(F32)
    below = below_ref[...].astype(F32)
    if edge:
        above = jnp.where(step == 0, halo_above_ref[...].astype(F32), above)
        below = jnp.where(step == steps - 1, halo_below_ref[...].astype(F32), below)

    ext = STRIP + 2
    store_halves(wide_scr, slice(0, 64), above)
    store_halves(wide_scr, slice(64, 64 + tokens), x_ref[...].astype(F32))
    store_halves(wide_scr, slice(64 + tokens, 128 + tokens), below)
    where_in = lax.broadcasted_iota(jnp.int32, (ext, 8, 256), 1)
    scale = (GELU_S * scale_ref[...])[None]
    shift = (GELU_S * shift_ref[...])[None]

    def paired(cells):
        both = jnp.stack([cells[:10], cells[8:18]], axis=1)
        return (both * scale[None] + shift[None]).reshape(160, 256).astype(BF16)

    def side(which):
        rows = side_scr[which, pl.ds(pl.multiple_of(step * 24, 8), 24), :]
        return jnp.broadcast_to(rows[:ext, None, :], (ext, 8, 256))

    slots = [None] * 10
    for low in range(8):
        cells = load_halves(wide_scr, pl.ds(low, ext * 8, stride=8))
        slots[low + 1] = paired(cells.reshape(ext, 8, 256))
        if low == 7:
            rolled = pltpu.roll(cells, 1, 0).reshape(ext, 8, 256)
            slots[0] = paired(jnp.where(where_in == 0, side(0), rolled))
        if low == 0:
            rolled = pltpu.roll(cells, ext * 8 - 1, 0).reshape(ext, 8, 256)
            slots[9] = paired(jnp.where(where_in == 7, side(1), rolled))

    sub = lax.broadcasted_iota(jnp.int32, (16, 256), 0)

    def keep(condition, outside):
        value = jnp.where(outside, 0.0, 1.0)
        return jnp.where(condition, value, 1.0).astype(BF16)

    row, rows_of = lax.axis_index(ROW), lax.axis_size(ROW)
    col, cols_of = lax.axis_index("col"), lax.axis_size("col")
    if edge:
        top = keep(sub < 8, jnp.logical_and(step == 0, row == 0))
        bottom = keep(sub >= 8, jnp.logical_and(step == steps - 1, row == rows_of - 1))
    at_left = keep(sub % 8 == 0, col == 0)
    at_right = keep(sub % 8 == 7, col == cols_of - 1)

    product = [None] * 8
    for cut in range(0, inner, 256):
        here = slice(cut, cut + 256)
        bias = (GELU_S * expand_bias_ref[:, here]).astype(BF16)
        cells = []
        for slot in range(10):
            one = scaled_gelu(dot(slots[slot], expand_ref[:, here]).astype(BF16) + bias)
            one = one.reshape(10, 16, 256)
            if edge:
                one = jnp.concatenate(
                    [one[:1] * top[None], one[1:9], one[9:] * bottom[None]], axis=0
                )
            if slot == 0:
                one = one * at_left[None]
            if slot == 9:
                one = one * at_right[None]
            cells.append(one)
        taps = [(GELU_S * GELU_BACK * depth_ref[k][:, here]).astype(BF16) for k in range(3)]
        depth_bias = (GELU_S * depth_bias_ref[:, here]).astype(BF16)
        for low in range(8):
            total = depth_bias[None]
            for s in range(3):
                for t in range(3):
                    tap = taps[s][t : t + 1][None]
                    total = total + cells[low + t][s : s + 8] * tap
            part = dot(scaled_gelu(total).reshape(128, 256), project_ref[here, :])
            product[low] = part if product[low] is None else product[low] + part
    for low in range(8):
        store_halves(prod_scr, slice(low * 128, (low + 1) * 128), product[low])
    pieces = []
    for w in range(16):
        for y in range(8):
            pieces.append(load_halves(prod_scr, pl.ds(y * 16 + w, 8, stride=128)))
    source = x_ref[...].astype(F32)
    source = source.reshape(2, 8, 8, 8, 256).swapaxes(1, 2).reshape(tokens, 256)
    rows = (source + GELU_BACK * jnp.concatenate(pieces, axis=0)).astype(BF16).astype(F32)
    done = attend_rows(
        rows, gains_ref, entry_ref, leave_ref, widen_ref, shrink_ref, offs_scr
    )
    done = done.reshape(2, 8, 8, 8, 256).swapaxes(1, 2).reshape(tokens, 256)
    out_ref[...] = done.astype(BF16)


def grid_kernel(
    x_ref,
    gains_ref,
    entry_ref,
    leave_ref,
    offsets_ref,
    widen_ref,
    shrink_ref,
    out_ref,
    in_scr,
    back_scr,
    offs_scr,
):
    @pl.when(pl.program_id(0) == 0)
    def _():
        prepare_offsets(offsets_ref, offs_scr)

    count = x_ref.shape[1]
    tokens = count * 64
    store_halves(in_scr, slice(0, tokens), x_ref[...].astype(F32).reshape(tokens, 256))
    rows = jnp.concatenate(
        [load_halves(in_scr, pl.ds(w, 64, stride=count)) for w in range(count)], axis=0
    )
    done = attend_rows(
        rows, gains_ref, entry_ref, leave_ref, widen_ref, shrink_ref, offs_scr
    )
    for w in range(count):
        store_halves(back_scr, pl.ds(w, 64, stride=count), done[w * 64 : (w + 1) * 64])
    out_ref[...] = load_halves(back_scr, slice(0, tokens)).reshape(64, count, 256).astype(BF16)


def attend_scratch():
    return [pltpu.VMEM((64, 512), F32)]


def whole(shape):
    return pl.BlockSpec(shape, lambda i: (0,) * len(shape))


def conv_block(x, body, above, below, halos, left, right, weights):
    channels = x.shape[1]
    steps = 2
    tokens = STRIP * 64
    row = (64, channels)
    return pl.pallas_call(
        functools.partial(conv_block_kernel, bool(halos)),
        grid=(steps,),
        in_specs=[
            pl.BlockSpec((tokens, channels), lambda i: (body(i), 0)),
            pl.BlockSpec(row, lambda i: (above(i), 0)),
            pl.BlockSpec(row, lambda i: (below(i), 0)),
        ]
        + [whole(h.shape) for h in halos]
        + [whole(left.shape), whole(right.shape)]
        + [whole(w.shape) for w in weights],
        out_specs=pl.BlockSpec((tokens, channels), lambda i: (i, 0)),
        out_shape=jax.ShapeDtypeStruct((steps * tokens, channels), BF16),
        scratch_shapes=[
            pltpu.VMEM((2, (STRIP + 2) * 64, 128), F32),
            pltpu.VMEM((2, 48, channels), F32),
            pltpu.VMEM((2, tokens, 128), F32),
            pltpu.VMEM((64, 512), F32),
        ],
        compiler_params=pltpu.CompilerParams(vmem_limit_bytes=56 << 20),
        cost_estimate=pl.CostEstimate(
            flops=steps * tokens * 7000000,
            bytes_accessed=steps * tokens * 1024 + 4000000,
            transcendentals=0,
        ),
        name="conv_block",
    )(x, x, x, *halos, left, right, *weights)


def grid_attend(x, weights):
    sources, count, channels = x.shape
    block = pl.BlockSpec((sources, GRID_WINDOWS, channels), lambda i: (0, i, 0))
    tokens = sources * GRID_WINDOWS
    return pl.pallas_call(
        grid_kernel,
        grid=(count // GRID_WINDOWS,),
        in_specs=[block] + [whole(w.shape) for w in weights],
        out_specs=block,
        out_shape=jax.ShapeDtypeStruct(x.shape, BF16),
        scratch_shapes=[
            pltpu.VMEM((2, tokens, 128), F32),
            pltpu.VMEM((2, tokens, 128), F32),
            pltpu.VMEM((64, 512), F32),
        ],
        compiler_params=pltpu.CompilerParams(vmem_limit_bytes=56 << 20),
        cost_estimate=pl.CostEstimate(
            flops=sources * count * 5000000,
            bytes_accessed=sources * count * 1024 + 4000000,
            transcendentals=0,
        ),
        name="grid_attend",
    )(x, *weights)


ROW = ("row_hi", "core")
GROUP = ("row_hi", "col")


def shards(
    radar_tiles,
    conv_scale,
    conv_shift,
    expand_weight,
    expand_bias,
    depth_kernel,
    depth_bias,
    project_weight,
    block_gains,
    block_entry,
    block_leave,
    block_offsets,
    block_widen,
    block_shrink,
    grid_gains,
    grid_entry,
    grid_leave,
    grid_offsets,
    grid_widen,
    grid_shrink,
):
    rows_here, cols_here, channels = radar_tiles.shape
    row_count, col_count = lax.axis_size(ROW), lax.axis_size("col")

    def shifted(values, axis, count, step):
        pairs = [(i, i + step) for i in range(count) if 0 <= i + step < count]
        return lax.ppermute(values, axis, pairs)

    x = radar_tiles.reshape(rows_here * cols_here, channels)
    above = shifted(x[-cols_here:], ROW, row_count, 1)
    below = shifted(x[:cols_here], ROW, row_count, -1)
    edges = [
        jnp.concatenate([above[e][None], radar_tiles[:, e], below[e][None]], axis=0)
        for e in (-1, 0)
    ]
    left = shifted(edges[0], "col", col_count, 1)
    right = shifted(edges[1], "col", col_count, -1)
    weights = (
        conv_scale.reshape(1, -1),
        conv_shift.reshape(1, -1),
        expand_weight,
        expand_bias.reshape(1, -1),
        depth_kernel,
        depth_bias.reshape(1, -1),
        project_weight,
        block_gains,
        block_entry,
        block_leave,
        block_offsets,
        block_widen,
        block_shrink,
    )
    grid_weights = (grid_gains, grid_entry, grid_leave, grid_offsets, grid_widen, grid_shrink)
    group = row_count // 2 * col_count
    blocks = rows_here // STRIP
    inner = conv_block(
        x,
        lambda i: i + 1,
        lambda i: STRIP * (i + 1) - 1,
        lambda i: STRIP * (i + 2),
        (),
        left,
        right,
        weights,
    )

    def spread(values):
        values = values.reshape(group, -1, channels)
        return lax.all_to_all(values, GROUP, split_axis=0, concat_axis=0, tiled=True)

    inner_there = spread(inner)
    outer = conv_block(
        x,
        lambda i: (blocks - 1) * i,
        lambda i: (rows_here - STRIP - 1) * i,
        lambda i: STRIP + (rows_here - STRIP - 1) * i,
        (above, below),
        left,
        right,
        weights,
    )
    outer_there = spread(outer)
    inner_back = spread(grid_attend(inner_there, grid_weights)).reshape(-1, cols_here, channels)
    outer_back = spread(grid_attend(outer_there, grid_weights)).reshape(-1, cols_here, channels)
    return jnp.concatenate([outer_back[:STRIP], inner_back, outer_back[STRIP:]], axis=0)


def solution(mesh):
    inner = Mesh(mesh.devices.reshape(8, 2, 8), ("row_hi", "core", "col"))
    tiles = P(ROW, "col", None)
    return jax.shard_map(
        shards,
        mesh=inner,
        in_specs=(tiles,) + (P(),) * 19,
        out_specs=tiles,
        check_vma=False,
    )
```

```python
import functools
import math

import jax
import jax.numpy as jnp
from jax import lax
from jax.experimental import pallas as pl
from jax.experimental.pallas import tpu as pltpu
from jax.sharding import Mesh, PartitionSpec as P

WIN = 8
STRIP = 16
GRID_WINDOWS = 16
epsilon = 1e-05
F32 = jnp.float32
BF16 = jnp.bfloat16
GELU_A = math.sqrt(2.0 / math.pi)
GELU_B = GELU_A * 0.044715
LOG2E = math.log2(math.e)


GELU_S = GELU_B ** (1.0 / 3.0)
GELU_C = GELU_A / GELU_S
GELU_BACK = 0.5 / GELU_S


def scaled_gelu(z):
    return z + z * jnp.tanh(z * (z * z + GELU_C))


def dot(a, b):
    return jnp.dot(a, b, preferred_element_type=F32)


def load_halves(ref, where):
    return jnp.concatenate([ref[0, where, :], ref[1, where, :]], axis=-1)


def store_halves(ref, where, values):
    ref[0, where, :] = values[:, :128]
    ref[1, where, :] = values[:, 128:]


def layer_norm(values, gain):
    mean = jnp.mean(values, axis=-1, keepdims=True)
    center = values - mean
    spread = jnp.mean(center * center, axis=-1, keepdims=True)
    return (center * lax.rsqrt(spread + epsilon) * gain).astype(BF16)


def halves_dot(a, b):
    half = a.shape[0] // 2
    return jnp.concatenate([dot(a[:half], b), dot(a[half:], b)], axis=0)


def prepare_offsets(table_ref, offs_scr):
    heads = table_ref.shape[0]
    for pair in range(heads // 2):
        two = jnp.concatenate([table_ref[2 * pair], table_ref[2 * pair + 1]], axis=-1)
        offs_scr[:, pair * 128 : (pair + 1) * 128] = two * LOG2E


def attend_rows(rows, gains_ref, entry_ref, leave_ref, offs_scr):
    count, channels = rows.shape
    windows = count // 64
    normed = layer_norm(rows, gains_ref[0:1, :])
    scale = LOG2E / math.sqrt(32.0)
    qkv = [
        halves_dot(normed, entry_ref[:, part * channels : (part + 1) * channels])
        for part in range(3)
    ]
    queries = (qkv[0] * scale).astype(BF16)
    keys = qkv[1].astype(BF16)
    values = qkv[2].astype(BF16)
    lane = lax.broadcasted_iota(jnp.int32, (64, 128), 1) // 32
    masks = [(lane == h).astype(F32).astype(BF16) for h in range(4)]
    key_head = lax.broadcasted_iota(jnp.int32, (256, 256), 0) // 64
    out_head = lax.broadcasted_iota(jnp.int32, (256, 256), 1) // 64
    adder = (key_head == out_head).astype(F32).astype(BF16)
    sides = []
    for g in range(2):
        part = slice(g * 128, (g + 1) * 128)
        wide_part = slice(g * 256, (g + 1) * 256)
        probs = []
        for w in range(windows):
            here = slice(w * 64, (w + 1) * 64)
            wide = jnp.concatenate([keys[here, part] * m for m in masks], axis=0)
            score = lax.dot_general(
                queries[here, part], wide, (((1,), (1,)), ((), ())), preferred_element_type=F32
            )
            probs.append(jnp.exp2(score + offs_scr[:, wide_part]))
        prob = jnp.concatenate(probs, axis=0)
        total = halves_dot(prob.astype(BF16), adder)
        weight = (prob / total).astype(BF16)
        mixed = []
        for w in range(windows):
            here = slice(w * 64, (w + 1) * 64)
            wide = jnp.concatenate([values[here, part] * m for m in masks], axis=0)
            mixed.append(dot(weight[here], wide).astype(BF16))
        sides.append(jnp.concatenate(mixed, axis=0))
    mixture = jnp.concatenate(sides, axis=-1)
    return (rows + halves_dot(mixture, leave_ref[...])).astype(BF16).astype(F32)


def feed_forward(attended, gains_ref, widen_ref, shrink_ref):
    second = layer_norm(attended, GELU_S * gains_ref[1:2, :])
    inner = widen_ref.shape[1]
    hidden = jnp.concatenate(
        [
            scaled_gelu(halves_dot(second, widen_ref[:, cut : cut + 256]).astype(BF16))
            for cut in range(0, inner, 256)
        ],
        axis=-1,
    )
    return (attended + GELU_BACK * halves_dot(hidden, shrink_ref[...])).astype(BF16)


def conv_block_kernel(edge, x_ref, above_ref, below_ref, *refs):
    if edge:
        halo_above_ref, halo_below_ref = refs[:2]
        refs = refs[2:]
    (
        left_ref,
        right_ref,
        scale_ref,
        shift_ref,
        expand_ref,
        expand_bias_ref,
        depth_ref,
        depth_bias_ref,
        project_ref,
        gains_ref,
        entry_ref,
        leave_ref,
        offsets_ref,
        out_ref,
        wide_scr,
        side_scr,
        prod_scr,
        offs_scr,
    ) = refs
    step = pl.program_id(0)
    steps = pl.num_programs(0)
    tokens = STRIP * 64
    inner = expand_ref.shape[1]

    @pl.when(step == 0)
    def _():
        prepare_offsets(offsets_ref, offs_scr)
        for which, ref in enumerate((left_ref, right_ref)):
            side = ref[...].astype(F32)
            first = 0 if edge else STRIP
            second = side.shape[0] - STRIP - 2 - first
            side_scr[which, 0:18, :] = side[first : first + 18]
            side_scr[which, 24:42, :] = side[second : second + 18]

    above = above_ref[...].astype(F32)
    below = below_ref[...].astype(F32)
    if edge:
        above = jnp.where(step == 0, halo_above_ref[...].astype(F32), above)
        below = jnp.where(step == steps - 1, halo_below_ref[...].astype(F32), below)

    ext = STRIP + 2
    store_halves(wide_scr, slice(0, 64), above)
    store_halves(wide_scr, slice(64, 64 + tokens), x_ref[...].astype(F32))
    store_halves(wide_scr, slice(64 + tokens, 128 + tokens), below)
    where_in = lax.broadcasted_iota(jnp.int32, (ext, 8, 256), 1)
    scale = (GELU_S * scale_ref[...])[None]
    shift = (GELU_S * shift_ref[...])[None]

    def paired(cells):
        both = jnp.stack([cells[:10], cells[8:18]], axis=1)
        return (both * scale[None] + shift[None]).reshape(160, 256).astype(BF16)

    def side(which):
        rows = side_scr[which, pl.ds(pl.multiple_of(step * 24, 8), 24), :]
        return jnp.broadcast_to(rows[:ext, None, :], (ext, 8, 256))

    slots = [None] * 10
    for low in range(8):
        cells = load_halves(wide_scr, pl.ds(low, ext * 8, stride=8))
        slots[low + 1] = paired(cells.reshape(ext, 8, 256))
        if low == 7:
            rolled = pltpu.roll(cells, 1, 0).reshape(ext, 8, 256)
            slots[0] = paired(jnp.where(where_in == 0, side(0), rolled))
        if low == 0:
            rolled = pltpu.roll(cells, ext * 8 - 1, 0).reshape(ext, 8, 256)
            slots[9] = paired(jnp.where(where_in == 7, side(1), rolled))

    sub = lax.broadcasted_iota(jnp.int32, (16, 256), 0)

    def keep(condition, outside):
        value = jnp.where(outside, 0.0, 1.0)
        return jnp.where(condition, value, 1.0).astype(BF16)

    row, rows_of = lax.axis_index(ROW), lax.axis_size(ROW)
    col, cols_of = lax.axis_index("col"), lax.axis_size("col")
    if edge:
        top = keep(sub < 8, jnp.logical_and(step == 0, row == 0))
        bottom = keep(sub >= 8, jnp.logical_and(step == steps - 1, row == rows_of - 1))
    at_left = keep(sub % 8 == 0, col == 0)
    at_right = keep(sub % 8 == 7, col == cols_of - 1)

    product = [None] * 8
    for cut in range(0, inner, 256):
        here = slice(cut, cut + 256)
        bias = (GELU_S * expand_bias_ref[:, here]).astype(BF16)
        cells = []
        for slot in range(10):
            one = scaled_gelu(dot(slots[slot], expand_ref[:, here]).astype(BF16) + bias)
            one = one.reshape(10, 16, 256)
            if edge:
                one = jnp.concatenate(
                    [one[:1] * top[None], one[1:9], one[9:] * bottom[None]], axis=0
                )
            if slot == 0:
                one = one * at_left[None]
            if slot == 9:
                one = one * at_right[None]
            cells.append(one)
        taps = [(GELU_S * GELU_BACK * depth_ref[k][:, here]).astype(BF16) for k in range(3)]
        depth_bias = (GELU_S * depth_bias_ref[:, here]).astype(BF16)
        for low in range(8):
            total = depth_bias[None]
            for s in range(3):
                for t in range(3):
                    tap = taps[s][t : t + 1][None]
                    total = total + cells[low + t][s : s + 8] * tap
            part = dot(scaled_gelu(total).reshape(128, 256), project_ref[here, :])
            product[low] = part if product[low] is None else product[low] + part
    for low in range(8):
        store_halves(prod_scr, slice(low * 128, (low + 1) * 128), product[low])
    pieces = []
    for w in range(16):
        for y in range(8):
            pieces.append(load_halves(prod_scr, pl.ds(y * 16 + w, 8, stride=128)))
    source = x_ref[...].astype(F32)
    source = source.reshape(2, 8, 8, 8, 256).swapaxes(1, 2).reshape(tokens, 256)
    rows = (source + GELU_BACK * jnp.concatenate(pieces, axis=0)).astype(BF16).astype(F32)
    done = attend_rows(rows, gains_ref, entry_ref, leave_ref, offs_scr)
    done = done.reshape(2, 8, 8, 8, 256).swapaxes(1, 2).reshape(tokens, 256)
    out_ref[...] = done.astype(BF16)


def grid_kernel(
    x_ref,
    before_gains_ref,
    before_widen_ref,
    before_shrink_ref,
    gains_ref,
    entry_ref,
    leave_ref,
    offsets_ref,
    widen_ref,
    shrink_ref,
    out_ref,
    in_scr,
    back_scr,
    offs_scr,
):
    @pl.when(pl.program_id(0) == 0)
    def _():
        prepare_offsets(offsets_ref, offs_scr)

    count = x_ref.shape[1]
    tokens = count * 64
    came = x_ref[...].astype(F32).reshape(tokens, 256)
    came = feed_forward(came, before_gains_ref, before_widen_ref, before_shrink_ref)
    store_halves(in_scr, slice(0, tokens), came.astype(F32))
    rows = jnp.concatenate(
        [load_halves(in_scr, pl.ds(w, 64, stride=count)) for w in range(count)], axis=0
    )
    attended = attend_rows(rows, gains_ref, entry_ref, leave_ref, offs_scr)
    done = feed_forward(attended, gains_ref, widen_ref, shrink_ref).astype(F32)
    for w in range(count):
        store_halves(back_scr, pl.ds(w, 64, stride=count), done[w * 64 : (w + 1) * 64])
    out_ref[...] = load_halves(back_scr, slice(0, tokens)).reshape(64, count, 256).astype(BF16)


def whole(shape):
    return pl.BlockSpec(shape, lambda i: (0,) * len(shape))


def conv_block(x, body, above, below, halos, left, right, weights):
    channels = x.shape[1]
    steps = 2
    tokens = STRIP * 64
    row = (64, channels)
    return pl.pallas_call(
        functools.partial(conv_block_kernel, bool(halos)),
        grid=(steps,),
        in_specs=[
            pl.BlockSpec((tokens, channels), lambda i: (body(i), 0)),
            pl.BlockSpec(row, lambda i: (above(i), 0)),
            pl.BlockSpec(row, lambda i: (below(i), 0)),
        ]
        + [whole(h.shape) for h in halos]
        + [whole(left.shape), whole(right.shape)]
        + [whole(w.shape) for w in weights],
        out_specs=pl.BlockSpec((tokens, channels), lambda i: (i, 0)),
        out_shape=jax.ShapeDtypeStruct((steps * tokens, channels), BF16),
        scratch_shapes=[
            pltpu.VMEM((2, (STRIP + 2) * 64, 128), F32),
            pltpu.VMEM((2, 48, channels), F32),
            pltpu.VMEM((2, tokens, 128), F32),
            pltpu.VMEM((64, 512), F32),
        ],
        compiler_params=pltpu.CompilerParams(vmem_limit_bytes=56 << 20),
        cost_estimate=pl.CostEstimate(
            flops=steps * tokens * 7000000,
            bytes_accessed=steps * tokens * 1024 + 4000000,
            transcendentals=0,
        ),
        name="conv_block",
    )(x, x, x, *halos, left, right, *weights)


def grid_attend(x, weights):
    sources, count, channels = x.shape
    block = pl.BlockSpec((sources, GRID_WINDOWS, channels), lambda i: (0, i, 0))
    tokens = sources * GRID_WINDOWS
    return pl.pallas_call(
        grid_kernel,
        grid=(count // GRID_WINDOWS,),
        in_specs=[block] + [whole(w.shape) for w in weights],
        out_specs=block,
        out_shape=jax.ShapeDtypeStruct(x.shape, BF16),
        scratch_shapes=[
            pltpu.VMEM((2, tokens, 128), F32),
            pltpu.VMEM((2, tokens, 128), F32),
            pltpu.VMEM((64, 512), F32),
        ],
        compiler_params=pltpu.CompilerParams(vmem_limit_bytes=56 << 20),
        cost_estimate=pl.CostEstimate(
            flops=sources * count * 5000000,
            bytes_accessed=sources * count * 1024 + 4000000,
            transcendentals=0,
        ),
        name="grid_attend",
    )(x, *weights)


ROW = ("row_hi", "core")
GROUP = ("row_hi", "col")


def shards(
    radar_tiles,
    conv_scale,
    conv_shift,
    expand_weight,
    expand_bias,
    depth_kernel,
    depth_bias,
    project_weight,
    block_gains,
    block_entry,
    block_leave,
    block_offsets,
    block_widen,
    block_shrink,
    grid_gains,
    grid_entry,
    grid_leave,
    grid_offsets,
    grid_widen,
    grid_shrink,
):
    rows_here, cols_here, channels = radar_tiles.shape
    row_count, col_count = lax.axis_size(ROW), lax.axis_size("col")

    def shifted(values, axis, count, step):
        pairs = [(i, i + step) for i in range(count) if 0 <= i + step < count]
        return lax.ppermute(values, axis, pairs)

    x = radar_tiles.reshape(rows_here * cols_here, channels)
    above = shifted(x[-cols_here:], ROW, row_count, 1)
    below = shifted(x[:cols_here], ROW, row_count, -1)
    edges = [
        jnp.concatenate([above[e][None], radar_tiles[:, e], below[e][None]], axis=0)
        for e in (-1, 0)
    ]
    left = shifted(edges[0], "col", col_count, 1)
    right = shifted(edges[1], "col", col_count, -1)
    weights = (
        conv_scale.reshape(1, -1),
        conv_shift.reshape(1, -1),
        expand_weight,
        expand_bias.reshape(1, -1),
        depth_kernel,
        depth_bias.reshape(1, -1),
        project_weight,
        block_gains,
        block_entry,
        block_leave,
        block_offsets,
    )
    grid_weights = (
        block_gains,
        block_widen,
        block_shrink,
        grid_gains,
        grid_entry,
        grid_leave,
        grid_offsets,
        grid_widen,
        grid_shrink,
    )
    group = row_count // 2 * col_count
    blocks = rows_here // STRIP
    inner = conv_block(
        x,
        lambda i: i + 1,
        lambda i: STRIP * (i + 1) - 1,
        lambda i: STRIP * (i + 2),
        (),
        left,
        right,
        weights,
    )

    def spread(values):
        values = values.reshape(group, -1, channels)
        return lax.all_to_all(values, GROUP, split_axis=0, concat_axis=0, tiled=True)

    inner_there = spread(inner)
    outer = conv_block(
        x,
        lambda i: (blocks - 1) * i,
        lambda i: (rows_here - STRIP - 1) * i,
        lambda i: STRIP + (rows_here - STRIP - 1) * i,
        (above, below),
        left,
        right,
        weights,
    )
    outer_there = spread(outer)
    inner_back = spread(grid_attend(inner_there, grid_weights)).reshape(-1, cols_here, channels)
    outer_back = spread(grid_attend(outer_there, grid_weights)).reshape(-1, cols_here, channels)
    return jnp.concatenate([outer_back[:STRIP], inner_back, outer_back[STRIP:]], axis=0)


def solution(mesh):
    inner = Mesh(mesh.devices.reshape(8, 2, 8), ("row_hi", "core", "col"))
    tiles = P(ROW, "col", None)
    return jax.shard_map(
        shards,
        mesh=inner,
        in_specs=(tiles,) + (P(),) * 19,
        out_specs=tiles,
        check_vma=False,
    )
```

```python
import functools
import math

import jax
import jax.numpy as jnp
from jax import lax
from jax.experimental import pallas as pl
from jax.experimental.pallas import tpu as pltpu
from jax.sharding import Mesh, PartitionSpec as P

WIN = 8
STRIP = 16
GRID_WINDOWS = 16
epsilon = 1e-05
F32 = jnp.float32
BF16 = jnp.bfloat16
GELU_A = math.sqrt(2.0 / math.pi)
GELU_B = GELU_A * 0.044715
LOG2E = math.log2(math.e)


GELU_S = GELU_B ** (1.0 / 3.0)
GELU_C = GELU_A / GELU_S
GELU_BACK = 0.5 / GELU_S


def scaled_gelu(z):
    return z + z * jnp.tanh(z * (z * z + GELU_C))


def dot(a, b):
    return jnp.dot(a, b, preferred_element_type=F32)


def load_halves(ref, where):
    return jnp.concatenate([ref[0, where, :], ref[1, where, :]], axis=-1)


def store_halves(ref, where, values):
    ref[0, where, :] = values[:, :128]
    ref[1, where, :] = values[:, 128:]


def layer_norm(values, gain):
    mean = jnp.mean(values, axis=-1, keepdims=True)
    center = values - mean
    spread = jnp.mean(center * center, axis=-1, keepdims=True)
    return (center * lax.rsqrt(spread + epsilon) * gain).astype(BF16)


def halves_dot(a, b):
    half = a.shape[0] // 2
    return jnp.concatenate([dot(a[:half], b), dot(a[half:], b)], axis=0)


def prepare_offsets(table_ref, offs_scr):
    heads = table_ref.shape[0]
    for pair in range(heads // 2):
        two = jnp.concatenate([table_ref[2 * pair], table_ref[2 * pair + 1]], axis=-1)
        offs_scr[:, pair * 128 : (pair + 1) * 128] = two * LOG2E


def attend_rows(rows, gains_ref, entry_ref, leave_ref, offs_scr):
    count, channels = rows.shape
    windows = count // 64
    normed = layer_norm(rows, gains_ref[0:1, :])
    scale = LOG2E / math.sqrt(32.0)
    qkv = [
        halves_dot(normed, entry_ref[:, part * channels : (part + 1) * channels])
        for part in range(3)
    ]
    queries = (qkv[0] * scale).astype(BF16)
    keys = qkv[1].astype(BF16)
    values = qkv[2].astype(BF16)
    lane = lax.broadcasted_iota(jnp.int32, (64, 128), 1) // 32
    masks = [(lane == h).astype(F32).astype(BF16) for h in range(4)]
    key_head = lax.broadcasted_iota(jnp.int32, (256, 256), 0) // 64
    out_head = lax.broadcasted_iota(jnp.int32, (256, 256), 1) // 64
    adder = (key_head == out_head).astype(F32).astype(BF16)
    sides = []
    for g in range(2):
        part = slice(g * 128, (g + 1) * 128)
        wide_part = slice(g * 256, (g + 1) * 256)
        probs = []
        for w in range(windows):
            here = slice(w * 64, (w + 1) * 64)
            wide = jnp.concatenate([keys[here, part] * m for m in masks], axis=0)
            score = lax.dot_general(
                queries[here, part], wide, (((1,), (1,)), ((), ())), preferred_element_type=F32
            )
            probs.append(jnp.exp2(score + offs_scr[:, wide_part]))
        prob = jnp.concatenate(probs, axis=0)
        total = halves_dot(prob.astype(BF16), adder)
        weight = (prob / total).astype(BF16)
        mixed = []
        for w in range(windows):
            here = slice(w * 64, (w + 1) * 64)
            wide = jnp.concatenate([values[here, part] * m for m in masks], axis=0)
            mixed.append(dot(weight[here], wide).astype(BF16))
        sides.append(jnp.concatenate(mixed, axis=0))
    mixture = jnp.concatenate(sides, axis=-1)
    return (rows + halves_dot(mixture, leave_ref[...])).astype(BF16).astype(F32)


def feed_forward(attended, gains_ref, widen_ref, shrink_ref):
    second = layer_norm(attended, GELU_S * gains_ref[1:2, :])
    inner = widen_ref.shape[1]
    hidden = jnp.concatenate(
        [
            scaled_gelu(halves_dot(second, widen_ref[:, cut : cut + 256]).astype(BF16))
            for cut in range(0, inner, 256)
        ],
        axis=-1,
    )
    return (attended + GELU_BACK * halves_dot(hidden, shrink_ref[...])).astype(BF16)


def conv_block_kernel(second_half, x_ref, above_ref, below_ref, *refs):
    halo_ref, *refs = refs
    (
        left_ref,
        right_ref,
        scale_ref,
        shift_ref,
        expand_ref,
        expand_bias_ref,
        depth_ref,
        depth_bias_ref,
        project_ref,
        gains_ref,
        entry_ref,
        leave_ref,
        offsets_ref,
        out_ref,
        wide_scr,
        side_scr,
        prod_scr,
        offs_scr,
    ) = refs
    step = pl.program_id(0)
    steps = pl.num_programs(0)
    tokens = STRIP * 64
    inner = expand_ref.shape[1]

    @pl.when(step == 0)
    def _():
        prepare_offsets(offsets_ref, offs_scr)
        for which, ref in enumerate((left_ref, right_ref)):
            side = ref[...].astype(F32)
            for part in range(2):
                first = (2 * second_half + part) * STRIP
                side_scr[which, 24 * part : 24 * part + 18, :] = side[first : first + 18]

    above = above_ref[...].astype(F32)
    below = below_ref[...].astype(F32)
    halo = halo_ref[...].astype(F32)
    if second_half:
        below = jnp.where(step == steps - 1, halo, below)
    else:
        above = jnp.where(step == 0, halo, above)

    ext = STRIP + 2
    store_halves(wide_scr, slice(0, 64), above)
    store_halves(wide_scr, slice(64, 64 + tokens), x_ref[...].astype(F32))
    store_halves(wide_scr, slice(64 + tokens, 128 + tokens), below)
    where_in = lax.broadcasted_iota(jnp.int32, (ext, 8, 256), 1)
    scale = (GELU_S * scale_ref[...])[None]
    shift = (GELU_S * shift_ref[...])[None]

    def paired(cells):
        both = jnp.stack([cells[:10], cells[8:18]], axis=1)
        return (both * scale[None] + shift[None]).reshape(160, 256).astype(BF16)

    def side(which):
        rows = side_scr[which, pl.ds(pl.multiple_of(step * 24, 8), 24), :]
        return jnp.broadcast_to(rows[:ext, None, :], (ext, 8, 256))

    slots = [None] * 10
    for low in range(8):
        cells = load_halves(wide_scr, pl.ds(low, ext * 8, stride=8))
        slots[low + 1] = paired(cells.reshape(ext, 8, 256))
        if low == 7:
            rolled = pltpu.roll(cells, 1, 0).reshape(ext, 8, 256)
            slots[0] = paired(jnp.where(where_in == 0, side(0), rolled))
        if low == 0:
            rolled = pltpu.roll(cells, ext * 8 - 1, 0).reshape(ext, 8, 256)
            slots[9] = paired(jnp.where(where_in == 7, side(1), rolled))

    sub = lax.broadcasted_iota(jnp.int32, (16, 256), 0)

    def keep(condition, outside):
        value = jnp.where(outside, 0.0, 1.0)
        return jnp.where(condition, value, 1.0).astype(BF16)

    row, rows_of = lax.axis_index(ROW), lax.axis_size(ROW)
    col, cols_of = lax.axis_index("col"), lax.axis_size("col")
    if second_half:
        border = keep(sub >= 8, jnp.logical_and(step == steps - 1, row == rows_of - 1))
    else:
        border = keep(sub < 8, jnp.logical_and(step == 0, row == 0))
    at_left = keep(sub % 8 == 0, col == 0)
    at_right = keep(sub % 8 == 7, col == cols_of - 1)

    product = [None] * 8
    for cut in range(0, inner, 256):
        here = slice(cut, cut + 256)
        bias = (GELU_S * expand_bias_ref[:, here]).astype(BF16)
        cells = []
        for slot in range(10):
            one = scaled_gelu(dot(slots[slot], expand_ref[:, here]).astype(BF16) + bias)
            one = one.reshape(10, 16, 256)
            if second_half:
                one = jnp.concatenate([one[:9], one[9:] * border[None]], axis=0)
            else:
                one = jnp.concatenate([one[:1] * border[None], one[1:]], axis=0)
            if slot == 0:
                one = one * at_left[None]
            if slot == 9:
                one = one * at_right[None]
            cells.append(one)
        taps = [(GELU_S * GELU_BACK * depth_ref[k][:, here]).astype(BF16) for k in range(3)]
        depth_bias = (GELU_S * depth_bias_ref[:, here]).astype(BF16)
        for low in range(8):
            total = depth_bias[None]
            for s in range(3):
                for t in range(3):
                    tap = taps[s][t : t + 1][None]
                    total = total + cells[low + t][s : s + 8] * tap
            part = dot(scaled_gelu(total).reshape(128, 256), project_ref[here, :])
            product[low] = part if product[low] is None else product[low] + part
    for low in range(8):
        store_halves(prod_scr, slice(low * 128, (low + 1) * 128), product[low])
    pieces = []
    for w in range(16):
        for y in range(8):
            pieces.append(load_halves(prod_scr, pl.ds(y * 16 + w, 8, stride=128)))
    source = x_ref[...].astype(F32)
    source = source.reshape(2, 8, 8, 8, 256).swapaxes(1, 2).reshape(tokens, 256)
    rows = (source + GELU_BACK * jnp.concatenate(pieces, axis=0)).astype(BF16).astype(F32)
    done = attend_rows(rows, gains_ref, entry_ref, leave_ref, offs_scr)
    done = done.reshape(2, 8, 8, 8, 256).swapaxes(1, 2).reshape(tokens, 256)
    out_ref[...] = done.astype(BF16)


def grid_kernel(
    x_ref,
    before_gains_ref,
    before_widen_ref,
    before_shrink_ref,
    gains_ref,
    entry_ref,
    leave_ref,
    offsets_ref,
    widen_ref,
    shrink_ref,
    out_ref,
    in_scr,
    back_scr,
    offs_scr,
):
    @pl.when(pl.program_id(0) == 0)
    def _():
        prepare_offsets(offsets_ref, offs_scr)

    count = x_ref.shape[1]
    tokens = count * 64
    came = x_ref[...].astype(F32).reshape(tokens, 256)
    came = feed_forward(came, before_gains_ref, before_widen_ref, before_shrink_ref)
    store_halves(in_scr, slice(0, tokens), came.astype(F32))
    rows = jnp.concatenate(
        [load_halves(in_scr, pl.ds(w, 64, stride=count)) for w in range(count)], axis=0
    )
    attended = attend_rows(rows, gains_ref, entry_ref, leave_ref, offs_scr)
    done = feed_forward(attended, gains_ref, widen_ref, shrink_ref).astype(F32)
    for w in range(count):
        store_halves(back_scr, pl.ds(w, 64, stride=count), done[w * 64 : (w + 1) * 64])
    out_ref[...] = load_halves(back_scr, slice(0, tokens)).reshape(64, count, 256).astype(BF16)


def whole(shape):
    return pl.BlockSpec(shape, lambda i: (0,) * len(shape))


def conv_block(second_half, x, halo, left, right, weights):
    tokens, channels = STRIP * 64, x.shape[1]
    blocks = x.shape[0] // tokens
    steps = blocks // 2
    row = (64, channels)
    base = steps * second_half

    def above(i):
        return jnp.maximum(STRIP * (base + i) - 1, 0)

    def below(i):
        return jnp.minimum(STRIP * (base + i + 1), STRIP * blocks - 1)

    return pl.pallas_call(
        functools.partial(conv_block_kernel, second_half),
        grid=(steps,),
        in_specs=[
            pl.BlockSpec((tokens, channels), lambda i: (base + i, 0)),
            pl.BlockSpec(row, lambda i: (above(i), 0)),
            pl.BlockSpec(row, lambda i: (below(i), 0)),
        ]
        + [whole(halo.shape), whole(left.shape), whole(right.shape)]
        + [whole(w.shape) for w in weights],
        out_specs=pl.BlockSpec((tokens, channels), lambda i: (i, 0)),
        out_shape=jax.ShapeDtypeStruct((steps * tokens, channels), BF16),
        scratch_shapes=[
            pltpu.VMEM((2, (STRIP + 2) * 64, 128), F32),
            pltpu.VMEM((2, 48, channels), F32),
            pltpu.VMEM((2, tokens, 128), F32),
            pltpu.VMEM((64, 512), F32),
        ],
        compiler_params=pltpu.CompilerParams(vmem_limit_bytes=56 << 20),
        cost_estimate=pl.CostEstimate(
            flops=steps * tokens * 7000000,
            bytes_accessed=steps * tokens * 1024 + 4000000,
            transcendentals=0,
        ),
        name="conv_block",
    )(x, x, x, halo, left, right, *weights)


def grid_attend(x, weights):
    sources, count, channels = x.shape
    block = pl.BlockSpec((sources, GRID_WINDOWS, channels), lambda i: (0, i, 0))
    tokens = sources * GRID_WINDOWS
    return pl.pallas_call(
        grid_kernel,
        grid=(count // GRID_WINDOWS,),
        in_specs=[block] + [whole(w.shape) for w in weights],
        out_specs=block,
        out_shape=jax.ShapeDtypeStruct(x.shape, BF16),
        scratch_shapes=[
            pltpu.VMEM((2, tokens, 128), F32),
            pltpu.VMEM((2, tokens, 128), F32),
            pltpu.VMEM((64, 512), F32),
        ],
        compiler_params=pltpu.CompilerParams(vmem_limit_bytes=56 << 20),
        cost_estimate=pl.CostEstimate(
            flops=sources * count * 5000000,
            bytes_accessed=sources * count * 1024 + 4000000,
            transcendentals=0,
        ),
        name="grid_attend",
    )(x, *weights)


ROW = ("row_hi", "core")
GROUP = ("row_hi", "col")


def shards(
    radar_tiles,
    conv_scale,
    conv_shift,
    expand_weight,
    expand_bias,
    depth_kernel,
    depth_bias,
    project_weight,
    block_gains,
    block_entry,
    block_leave,
    block_offsets,
    block_widen,
    block_shrink,
    grid_gains,
    grid_entry,
    grid_leave,
    grid_offsets,
    grid_widen,
    grid_shrink,
):
    rows_here, cols_here, channels = radar_tiles.shape
    row_count, col_count = lax.axis_size(ROW), lax.axis_size("col")

    def shifted(values, axis, count, step):
        pairs = [(i, i + step) for i in range(count) if 0 <= i + step < count]
        return lax.ppermute(values, axis, pairs)

    x = radar_tiles.reshape(rows_here * cols_here, channels)
    even = lax.axis_index("core") == 0
    top, bottom = x[:cols_here], x[-cols_here:]
    near = lax.ppermute(jnp.where(even, bottom, top), "core", [(0, 1), (1, 0)])
    ends = [(r, r + 1) for r in range(1, row_count - 1, 2)]
    far = lax.ppermute(jnp.where(even, top, bottom), ROW, ends + [(b, a) for a, b in ends])
    above = jnp.where(even, far, near)
    below = jnp.where(even, near, far)
    edges = [
        jnp.concatenate([above[e][None], radar_tiles[:, e], below[e][None]], axis=0)
        for e in (-1, 0)
    ]
    left = shifted(edges[0], "col", col_count, 1)
    right = shifted(edges[1], "col", col_count, -1)
    weights = (
        conv_scale.reshape(1, -1),
        conv_shift.reshape(1, -1),
        expand_weight,
        expand_bias.reshape(1, -1),
        depth_kernel,
        depth_bias.reshape(1, -1),
        project_weight,
        block_gains,
        block_entry,
        block_leave,
        block_offsets,
    )
    grid_weights = (
        block_gains,
        block_widen,
        block_shrink,
        grid_gains,
        grid_entry,
        grid_leave,
        grid_offsets,
        grid_widen,
        grid_shrink,
    )
    group = row_count // 2 * col_count
    def spread(values):
        values = values.reshape(group, -1, channels)
        return lax.all_to_all(values, GROUP, split_axis=0, concat_axis=0, tiled=True)

    upper_there = spread(conv_block(False, x, above, left, right, weights))
    lower_there = spread(conv_block(True, x, below, left, right, weights))
    half = (rows_here // 2, cols_here, channels)
    upper = spread(grid_attend(upper_there, grid_weights)).reshape(half)
    lower = spread(grid_attend(lower_there, grid_weights)).reshape(half)
    result = jnp.pad(upper, ((0, half[0]), (0, 0), (0, 0)))
    result = lax.optimization_barrier(result)
    return lax.dynamic_update_slice(result, lower, (half[0], 0, 0))


def solution(mesh):
    inner = Mesh(mesh.devices.reshape(8, 2, 8), ("row_hi", "core", "col"))
    tiles = P(ROW, "col", None)
    return jax.shard_map(
        shards,
        mesh=inner,
        in_specs=(tiles,) + (P(),) * 19,
        out_specs=tiles,
        check_vma=False,
    )
```

```python
import functools
import math

import jax
import jax.numpy as jnp
from jax import lax
from jax.experimental import pallas as pl
from jax.experimental.pallas import tpu as pltpu
from jax.sharding import Mesh, PartitionSpec as P

WIN = 8
STRIP = 16
GRID_WINDOWS = 16
epsilon = 1e-05
F32 = jnp.float32
BF16 = jnp.bfloat16
GELU_A = math.sqrt(2.0 / math.pi)
GELU_B = GELU_A * 0.044715
LOG2E = math.log2(math.e)


GELU_S = GELU_B ** (1.0 / 3.0)
GELU_C = GELU_A / GELU_S
GELU_BACK = 0.5 / GELU_S


def scaled_gelu(z):
    return z + z * jnp.tanh(z * (z * z + GELU_C))


def dot(a, b):
    return jnp.dot(a, b, preferred_element_type=F32)


def load_halves(ref, where):
    return jnp.concatenate([ref[0, where, :], ref[1, where, :]], axis=-1)


def store_halves(ref, where, values):
    ref[0, where, :] = values[:, :128]
    ref[1, where, :] = values[:, 128:]


def layer_norm(values, gain):
    mean = jnp.mean(values, axis=-1, keepdims=True)
    center = values - mean
    spread = jnp.mean(center * center, axis=-1, keepdims=True)
    return (center * lax.rsqrt(spread + epsilon) * gain).astype(BF16)


def halves_dot(a, b):
    half = a.shape[0] // 2
    return jnp.concatenate([dot(a[:half], b), dot(a[half:], b)], axis=0)


def prepare_offsets(table_ref, offs_scr):
    heads = table_ref.shape[0]
    for pair in range(heads // 2):
        two = jnp.concatenate([table_ref[2 * pair], table_ref[2 * pair + 1]], axis=-1)
        offs_scr[:, pair * 128 : (pair + 1) * 128] = two * LOG2E


def attend_rows(rows, gains_ref, entry_ref, leave_ref, offs_scr):
    count, channels = rows.shape
    windows = count // 64
    normed = layer_norm(rows, gains_ref[0:1, :])
    scale = LOG2E / math.sqrt(32.0)
    qkv = [
        halves_dot(normed, entry_ref[:, part * channels : (part + 1) * channels])
        for part in range(3)
    ]
    queries = (qkv[0] * scale).astype(BF16)
    keys = qkv[1].astype(BF16)
    values = qkv[2].astype(BF16)
    lane = lax.broadcasted_iota(jnp.int32, (64, 128), 1) // 32
    masks = [(lane == h).astype(F32).astype(BF16) for h in range(4)]
    key_head = lax.broadcasted_iota(jnp.int32, (256, 256), 0) // 64
    out_head = lax.broadcasted_iota(jnp.int32, (256, 256), 1) // 64
    adder = (key_head == out_head).astype(F32).astype(BF16)
    sides = []
    for g in range(2):
        part = slice(g * 128, (g + 1) * 128)
        wide_part = slice(g * 256, (g + 1) * 256)
        probs = []
        for w in range(windows):
            here = slice(w * 64, (w + 1) * 64)
            wide = jnp.concatenate([keys[here, part] * m for m in masks], axis=0)
            score = lax.dot_general(
                queries[here, part], wide, (((1,), (1,)), ((), ())), preferred_element_type=F32
            )
            probs.append(jnp.exp2(score + offs_scr[:, wide_part]))
        prob = jnp.concatenate(probs, axis=0)
        total = halves_dot(prob.astype(BF16), adder)
        weight = (prob / total).astype(BF16)
        mixed = []
        for w in range(windows):
            here = slice(w * 64, (w + 1) * 64)
            wide = jnp.concatenate([values[here, part] * m for m in masks], axis=0)
            mixed.append(dot(weight[here], wide).astype(BF16))
        sides.append(jnp.concatenate(mixed, axis=0))
    mixture = jnp.concatenate(sides, axis=-1)
    return (rows + halves_dot(mixture, leave_ref[...])).astype(BF16).astype(F32)


def feed_forward(attended, gains_ref, widen_ref, shrink_ref):
    second = layer_norm(attended, GELU_S * gains_ref[1:2, :])
    inner = widen_ref.shape[1]
    hidden = jnp.concatenate(
        [
            scaled_gelu(halves_dot(second, widen_ref[:, cut : cut + 256]).astype(BF16))
            for cut in range(0, inner, 256)
        ],
        axis=-1,
    )
    return (attended + GELU_BACK * halves_dot(hidden, shrink_ref[...])).astype(BF16)


def conv_block_kernel(second_half, x_ref, above_ref, below_ref, *refs):
    halo_ref, *refs = refs
    (
        left_ref,
        right_ref,
        scale_ref,
        shift_ref,
        expand_ref,
        expand_bias_ref,
        depth_ref,
        depth_bias_ref,
        project_ref,
        gains_ref,
        entry_ref,
        leave_ref,
        offsets_ref,
        out_ref,
        wide_scr,
        side_scr,
        prod_scr,
        offs_scr,
    ) = refs
    step = pl.program_id(0)
    steps = pl.num_programs(0)
    tokens = STRIP * 64
    inner = expand_ref.shape[1]

    @pl.when(step == 0)
    def _():
        prepare_offsets(offsets_ref, offs_scr)
        for which, ref in enumerate((left_ref, right_ref)):
            side = ref[...].astype(F32)
            for part in range(2):
                first = (2 * second_half + part) * STRIP
                side_scr[which, 24 * part : 24 * part + 18, :] = side[first : first + 18]

    above = above_ref[...].astype(F32)
    below = below_ref[...].astype(F32)
    halo = halo_ref[...].astype(F32)
    if second_half:
        below = jnp.where(step == steps - 1, halo, below)
    else:
        above = jnp.where(step == 0, halo, above)

    ext = STRIP + 2
    store_halves(wide_scr, slice(0, 64), above)
    store_halves(wide_scr, slice(64, 64 + tokens), x_ref[...].astype(F32))
    store_halves(wide_scr, slice(64 + tokens, 128 + tokens), below)
    where_in = lax.broadcasted_iota(jnp.int32, (ext, 8, 256), 1)
    scale = (GELU_S * scale_ref[...])[None]
    shift = (GELU_S * shift_ref[...])[None]

    def paired(cells):
        both = jnp.stack([cells[:10], cells[8:18]], axis=1)
        return (both * scale[None] + shift[None]).reshape(160, 256).astype(BF16)

    def side(which):
        rows = side_scr[which, pl.ds(pl.multiple_of(step * 24, 8), 24), :]
        return jnp.broadcast_to(rows[:ext, None, :], (ext, 8, 256))

    slots = [None] * 10
    for low in range(8):
        cells = load_halves(wide_scr, pl.ds(low, ext * 8, stride=8))
        slots[low + 1] = paired(cells.reshape(ext, 8, 256))
        if low == 7:
            rolled = pltpu.roll(cells, 1, 0).reshape(ext, 8, 256)
            slots[0] = paired(jnp.where(where_in == 0, side(0), rolled))
        if low == 0:
            rolled = pltpu.roll(cells, ext * 8 - 1, 0).reshape(ext, 8, 256)
            slots[9] = paired(jnp.where(where_in == 7, side(1), rolled))

    sub = lax.broadcasted_iota(jnp.int32, (16, 256), 0)

    def keep(condition, outside):
        value = jnp.where(outside, 0.0, 1.0)
        return jnp.where(condition, value, 1.0).astype(BF16)

    row, rows_of = lax.axis_index(ROW), lax.axis_size(ROW)
    col, cols_of = lax.axis_index("col"), lax.axis_size("col")
    if second_half:
        border = keep(sub >= 8, jnp.logical_and(step == steps - 1, row == rows_of - 1))
    else:
        border = keep(sub < 8, jnp.logical_and(step == 0, row == 0))
    at_left = keep(sub % 8 == 0, col == 0)
    at_right = keep(sub % 8 == 7, col == cols_of - 1)

    product = [None] * 8
    for cut in range(0, inner, 256):
        here = slice(cut, cut + 256)
        bias = (GELU_S * expand_bias_ref[:, here]).astype(BF16)
        cells = []
        for slot in range(10):
            one = scaled_gelu(dot(slots[slot], expand_ref[:, here]).astype(BF16) + bias)
            one = one.reshape(10, 16, 256)
            if second_half:
                one = jnp.concatenate([one[:9], one[9:] * border[None]], axis=0)
            else:
                one = jnp.concatenate([one[:1] * border[None], one[1:]], axis=0)
            if slot == 0:
                one = one * at_left[None]
            if slot == 9:
                one = one * at_right[None]
            cells.append(one)
        taps = [(GELU_S * GELU_BACK * depth_ref[k][:, here]).astype(BF16) for k in range(3)]
        depth_bias = (GELU_S * depth_bias_ref[:, here]).astype(BF16)
        for low in range(8):
            total = depth_bias[None]
            for s in range(3):
                for t in range(3):
                    tap = taps[s][t : t + 1][None]
                    total = total + cells[low + t][s : s + 8] * tap
            part = dot(scaled_gelu(total).reshape(128, 256), project_ref[here, :])
            product[low] = part if product[low] is None else product[low] + part
    for low in range(8):
        for strip in range(16):
            first = (strip * 8 + low) * 8
            store_halves(
                prod_scr, slice(first, first + 8), product[low][strip * 8 : strip * 8 + 8]
            )
    pieces = []
    for half in range(2):
        for w in range(8):
            for y in range(8):
                pieces.append(
                    load_halves(prod_scr, pl.ds((2 * y + half) * 64 + w, 8, stride=8))
                )
    source = x_ref[...].astype(F32)
    source = source.reshape(2, 8, 8, 8, 256).swapaxes(1, 2).reshape(tokens, 256)
    rows = (source + GELU_BACK * jnp.concatenate(pieces, axis=0)).astype(BF16).astype(F32)
    done = attend_rows(rows, gains_ref, entry_ref, leave_ref, offs_scr)
    done = done.reshape(2, 8, 8, 8, 256).swapaxes(1, 2).reshape(tokens, 256)
    out_ref[...] = done.astype(BF16)


def grid_kernel(
    x_ref,
    before_gains_ref,
    before_widen_ref,
    before_shrink_ref,
    gains_ref,
    entry_ref,
    leave_ref,
    offsets_ref,
    widen_ref,
    shrink_ref,
    out_ref,
    in_scr,
    back_scr,
    offs_scr,
):
    @pl.when(pl.program_id(0) == 0)
    def _():
        prepare_offsets(offsets_ref, offs_scr)

    count = x_ref.shape[1]
    tokens = count * 64
    came = x_ref[...].astype(F32).reshape(tokens, 256)
    came = feed_forward(came, before_gains_ref, before_widen_ref, before_shrink_ref)
    store_halves(in_scr, slice(0, tokens), came.astype(F32))
    rows = jnp.concatenate(
        [load_halves(in_scr, pl.ds(w, 64, stride=count)) for w in range(count)], axis=0
    )
    attended = attend_rows(rows, gains_ref, entry_ref, leave_ref, offs_scr)
    done = feed_forward(attended, gains_ref, widen_ref, shrink_ref).astype(F32)
    for w in range(count):
        store_halves(back_scr, pl.ds(w, 64, stride=count), done[w * 64 : (w + 1) * 64])
    out_ref[...] = load_halves(back_scr, slice(0, tokens)).reshape(64, count, 256).astype(BF16)


def whole(shape):
    return pl.BlockSpec(shape, lambda i: (0,) * len(shape))


def conv_block(second_half, x, halo, left, right, weights):
    tokens, channels = STRIP * 64, x.shape[1]
    blocks = x.shape[0] // tokens
    steps = blocks // 2
    row = (64, channels)
    base = steps * second_half

    def above(i):
        return jnp.maximum(STRIP * (base + i) - 1, 0)

    def below(i):
        return jnp.minimum(STRIP * (base + i + 1), STRIP * blocks - 1)

    return pl.pallas_call(
        functools.partial(conv_block_kernel, second_half),
        grid=(steps,),
        in_specs=[
            pl.BlockSpec((tokens, channels), lambda i: (base + i, 0)),
            pl.BlockSpec(row, lambda i: (above(i), 0)),
            pl.BlockSpec(row, lambda i: (below(i), 0)),
        ]
        + [whole(halo.shape), whole(left.shape), whole(right.shape)]
        + [whole(w.shape) for w in weights],
        out_specs=pl.BlockSpec((tokens, channels), lambda i: (i, 0)),
        out_shape=jax.ShapeDtypeStruct((steps * tokens, channels), BF16),
        scratch_shapes=[
            pltpu.VMEM((2, (STRIP + 2) * 64, 128), F32),
            pltpu.VMEM((2, 48, channels), F32),
            pltpu.VMEM((2, tokens, 128), F32),
            pltpu.VMEM((64, 512), F32),
        ],
        compiler_params=pltpu.CompilerParams(vmem_limit_bytes=56 << 20),
        cost_estimate=pl.CostEstimate(
            flops=steps * tokens * 7000000,
            bytes_accessed=steps * tokens * 1024 + 4000000,
            transcendentals=0,
        ),
        name="conv_block",
    )(x, x, x, halo, left, right, *weights)


def grid_attend(x, weights):
    sources, count, channels = x.shape
    block = pl.BlockSpec((sources, GRID_WINDOWS, channels), lambda i: (0, i, 0))
    tokens = sources * GRID_WINDOWS
    return pl.pallas_call(
        grid_kernel,
        grid=(count // GRID_WINDOWS,),
        in_specs=[block] + [whole(w.shape) for w in weights],
        out_specs=block,
        out_shape=jax.ShapeDtypeStruct(x.shape, BF16),
        scratch_shapes=[
            pltpu.VMEM((2, tokens, 128), F32),
            pltpu.VMEM((2, tokens, 128), F32),
            pltpu.VMEM((64, 512), F32),
        ],
        compiler_params=pltpu.CompilerParams(vmem_limit_bytes=56 << 20),
        cost_estimate=pl.CostEstimate(
            flops=sources * count * 5000000,
            bytes_accessed=sources * count * 1024 + 4000000,
            transcendentals=0,
        ),
        name="grid_attend",
    )(x, *weights)


ROW = ("row_hi", "core")
GROUP = ("row_hi", "col")


def shards(
    radar_tiles,
    conv_scale,
    conv_shift,
    expand_weight,
    expand_bias,
    depth_kernel,
    depth_bias,
    project_weight,
    block_gains,
    block_entry,
    block_leave,
    block_offsets,
    block_widen,
    block_shrink,
    grid_gains,
    grid_entry,
    grid_leave,
    grid_offsets,
    grid_widen,
    grid_shrink,
):
    rows_here, cols_here, channels = radar_tiles.shape
    row_count, col_count = lax.axis_size(ROW), lax.axis_size("col")

    def shifted(values, axis, count, step):
        pairs = [(i, i + step) for i in range(count) if 0 <= i + step < count]
        return lax.ppermute(values, axis, pairs)

    x = radar_tiles.reshape(rows_here * cols_here, channels)
    even = lax.axis_index("core") == 0
    top, bottom = x[:cols_here], x[-cols_here:]
    near = lax.ppermute(jnp.where(even, bottom, top), "core", [(0, 1), (1, 0)])
    ends = [(r, r + 1) for r in range(1, row_count - 1, 2)]
    far = lax.ppermute(jnp.where(even, top, bottom), ROW, ends + [(b, a) for a, b in ends])
    above = jnp.where(even, far, near)
    below = jnp.where(even, near, far)
    edges = [
        jnp.concatenate([above[e][None], radar_tiles[:, e], below[e][None]], axis=0)
        for e in (-1, 0)
    ]
    left = shifted(edges[0], "col", col_count, 1)
    right = shifted(edges[1], "col", col_count, -1)
    weights = (
        conv_scale.reshape(1, -1),
        conv_shift.reshape(1, -1),
        expand_weight,
        expand_bias.reshape(1, -1),
        depth_kernel,
        depth_bias.reshape(1, -1),
        project_weight,
        block_gains,
        block_entry,
        block_leave,
        block_offsets,
    )
    grid_weights = (
        block_gains,
        block_widen,
        block_shrink,
        grid_gains,
        grid_entry,
        grid_leave,
        grid_offsets,
        grid_widen,
        grid_shrink,
    )
    group = row_count // 2 * col_count
    def spread(values):
        values = values.reshape(group, -1, channels)
        return lax.all_to_all(values, GROUP, split_axis=0, concat_axis=0, tiled=True)

    upper_there = spread(conv_block(False, x, above, left, right, weights))
    lower_there = spread(conv_block(True, x, below, left, right, weights))
    half = (rows_here // 2, cols_here, channels)
    upper = spread(grid_attend(upper_there, grid_weights)).reshape(half)
    lower = spread(grid_attend(lower_there, grid_weights)).reshape(half)
    result = jnp.pad(upper, ((0, half[0]), (0, 0), (0, 0)))
    result = lax.optimization_barrier(result)
    return lax.dynamic_update_slice(result, lower, (half[0], 0, 0))


def solution(mesh):
    inner = Mesh(mesh.devices.reshape(8, 2, 8), ("row_hi", "core", "col"))
    tiles = P(ROW, "col", None)
    return jax.shard_map(
        shards,
        mesh=inner,
        in_specs=(tiles,) + (P(),) * 19,
        out_specs=tiles,
        check_vma=False,
    )
```

```python
import functools
import math

import jax
import jax.numpy as jnp
from jax import lax
from jax.experimental import pallas as pl
from jax.experimental.pallas import tpu as pltpu
from jax.sharding import Mesh, PartitionSpec as P

WIN = 8
STRIP = 16
GRID_WINDOWS = 16
epsilon = 1e-05
F32 = jnp.float32
BF16 = jnp.bfloat16
GELU_A = math.sqrt(2.0 / math.pi)
GELU_B = GELU_A * 0.044715
LOG2E = math.log2(math.e)


GELU_S = GELU_B ** (1.0 / 3.0)
GELU_C = GELU_A / GELU_S
GELU_BACK = 0.5 / GELU_S


def scaled_gelu(z):
    return z + z * jnp.tanh(z * (z * z + GELU_C))


def dot(a, b):
    return jnp.dot(a, b, preferred_element_type=F32)


def load_halves(ref, where):
    return jnp.concatenate([ref[0, where, :], ref[1, where, :]], axis=-1)


def store_halves(ref, where, values):
    ref[0, where, :] = values[:, :128]
    ref[1, where, :] = values[:, 128:]


def layer_norm(values, gain):
    mean = jnp.mean(values, axis=-1, keepdims=True)
    center = values - mean
    spread = jnp.mean(center * center, axis=-1, keepdims=True)
    return (center * lax.rsqrt(spread + epsilon) * gain).astype(BF16)


def halves_dot(a, b):
    half = a.shape[0] // 2
    return jnp.concatenate([dot(a[:half], b), dot(a[half:], b)], axis=0)


def prepare_offsets(table_ref, offs_scr):
    heads = table_ref.shape[0]
    for pair in range(heads // 2):
        two = jnp.concatenate([table_ref[2 * pair], table_ref[2 * pair + 1]], axis=-1)
        offs_scr[:, pair * 128 : (pair + 1) * 128] = two * LOG2E


def attend_rows(rows, gains_ref, entry_ref, leave_ref, offs_scr):
    count, channels = rows.shape
    windows = count // 64
    normed = layer_norm(rows, gains_ref[0:1, :])
    scale = LOG2E / math.sqrt(32.0)
    qkv = [
        halves_dot(normed, entry_ref[:, part * channels : (part + 1) * channels])
        for part in range(3)
    ]
    queries = (qkv[0] * scale).astype(BF16)
    keys = qkv[1].astype(BF16)
    values = qkv[2].astype(BF16)
    lane = lax.broadcasted_iota(jnp.int32, (64, 128), 1) // 32
    masks = [(lane == h).astype(F32).astype(BF16) for h in range(4)]
    key_head = lax.broadcasted_iota(jnp.int32, (256, 256), 0) // 64
    out_head = lax.broadcasted_iota(jnp.int32, (256, 256), 1) // 64
    adder = (key_head == out_head).astype(F32).astype(BF16)
    sides = []
    for g in range(2):
        part = slice(g * 128, (g + 1) * 128)
        wide_part = slice(g * 256, (g + 1) * 256)
        probs = []
        for w in range(windows):
            here = slice(w * 64, (w + 1) * 64)
            wide = jnp.concatenate([keys[here, part] * m for m in masks], axis=0)
            score = lax.dot_general(
                queries[here, part], wide, (((1,), (1,)), ((), ())), preferred_element_type=F32
            )
            probs.append(jnp.exp2(score + offs_scr[:, wide_part]))
        prob = jnp.concatenate(probs, axis=0)
        total = halves_dot(prob.astype(BF16), adder)
        weight = (prob / total).astype(BF16)
        mixed = []
        for w in range(windows):
            here = slice(w * 64, (w + 1) * 64)
            wide = jnp.concatenate([values[here, part] * m for m in masks], axis=0)
            mixed.append(dot(weight[here], wide).astype(BF16))
        sides.append(jnp.concatenate(mixed, axis=0))
    mixture = jnp.concatenate(sides, axis=-1)
    return (rows + halves_dot(mixture, leave_ref[...])).astype(BF16).astype(F32)


def feed_forward(attended, gains_ref, widen_ref, shrink_ref):
    second = layer_norm(attended, GELU_S * gains_ref[1:2, :])
    inner = widen_ref.shape[1]
    hidden = jnp.concatenate(
        [
            scaled_gelu(halves_dot(second, widen_ref[:, cut : cut + 256]).astype(BF16))
            for cut in range(0, inner, 256)
        ],
        axis=-1,
    )
    return (attended + GELU_BACK * halves_dot(hidden, shrink_ref[...])).astype(BF16)


def conv_block_kernel(second_half, x_ref, above_ref, below_ref, *refs):
    halo_ref, *refs = refs
    (
        left_ref,
        right_ref,
        scale_ref,
        shift_ref,
        expand_ref,
        expand_bias_ref,
        depth_ref,
        depth_bias_ref,
        project_ref,
        gains_ref,
        entry_ref,
        leave_ref,
        offsets_ref,
        out_ref,
        wide_scr,
        side_scr,
        prod_scr,
        offs_scr,
    ) = refs
    step = pl.program_id(0)
    steps = pl.num_programs(0)
    tokens = STRIP * 64
    inner = expand_ref.shape[1]

    @pl.when(step == 0)
    def _():
        prepare_offsets(offsets_ref, offs_scr)
        for which, ref in enumerate((left_ref, right_ref)):
            side = ref[...].astype(F32)
            for part in range(2):
                first = (2 * second_half + part) * STRIP
                side_scr[which, 24 * part : 24 * part + 18, :] = side[first : first + 18]

    above = above_ref[...].astype(F32)
    below = below_ref[...].astype(F32)
    halo = halo_ref[...].astype(F32)
    if second_half:
        below = jnp.where(step == steps - 1, halo, below)
    else:
        above = jnp.where(step == 0, halo, above)

    ext = STRIP + 2
    store_halves(wide_scr, slice(0, 64), above)
    store_halves(wide_scr, slice(64, 64 + tokens), x_ref[...].astype(F32))
    store_halves(wide_scr, slice(64 + tokens, 128 + tokens), below)
    where_in = lax.broadcasted_iota(jnp.int32, (ext, 8, 256), 1)
    scale = (GELU_S * scale_ref[...])[None]
    shift = (GELU_S * shift_ref[...])[None]

    def paired(cells):
        both = jnp.stack([cells[:10], cells[8:18]], axis=1)
        return (both * scale[None] + shift[None]).reshape(160, 256).astype(BF16)

    def side(which):
        rows = side_scr[which, pl.ds(pl.multiple_of(step * 24, 8), 24), :]
        return jnp.broadcast_to(rows[:ext, None, :], (ext, 8, 256))

    slots = [None] * 10
    for low in range(8):
        cells = load_halves(wide_scr, pl.ds(low, ext * 8, stride=8))
        slots[low + 1] = paired(cells.reshape(ext, 8, 256))
        if low == 7:
            rolled = pltpu.roll(cells, 1, 0).reshape(ext, 8, 256)
            slots[0] = paired(jnp.where(where_in == 0, side(0), rolled))
        if low == 0:
            rolled = pltpu.roll(cells, ext * 8 - 1, 0).reshape(ext, 8, 256)
            slots[9] = paired(jnp.where(where_in == 7, side(1), rolled))

    sub = lax.broadcasted_iota(jnp.int32, (16, 256), 0)

    def keep(condition, outside):
        value = jnp.where(outside, 0.0, 1.0)
        return jnp.where(condition, value, 1.0).astype(BF16)

    row, rows_of = lax.axis_index(ROW), lax.axis_size(ROW)
    col, cols_of = lax.axis_index("col"), lax.axis_size("col")
    if second_half:
        border = keep(sub >= 8, jnp.logical_and(step == steps - 1, row == rows_of - 1))
    else:
        border = keep(sub < 8, jnp.logical_and(step == 0, row == 0))
    at_left = keep(sub % 8 == 0, col == 0)
    at_right = keep(sub % 8 == 7, col == cols_of - 1)

    product = [None] * 8
    for cut in range(0, inner, 256):
        here = slice(cut, cut + 256)
        bias = (GELU_S * expand_bias_ref[:, here]).astype(BF16)
        cells = []
        for slot in range(10):
            one = scaled_gelu(dot(slots[slot], expand_ref[:, here]).astype(BF16) + bias)
            one = one.reshape(10, 16, 256)
            if second_half:
                one = jnp.concatenate([one[:9], one[9:] * border[None]], axis=0)
            else:
                one = jnp.concatenate([one[:1] * border[None], one[1:]], axis=0)
            if slot == 0:
                one = one * at_left[None]
            if slot == 9:
                one = one * at_right[None]
            cells.append(one)
        taps = [(GELU_S * GELU_BACK * depth_ref[k][:, here]).astype(BF16) for k in range(3)]
        depth_bias = (GELU_S * depth_bias_ref[:, here]).astype(BF16)
        for low in range(8):
            total = depth_bias[None]
            for s in range(3):
                for t in range(3):
                    tap = taps[s][t : t + 1][None]
                    total = total + cells[low + t][s : s + 8] * tap
            part = dot(scaled_gelu(total).reshape(128, 256), project_ref[here, :])
            product[low] = part if product[low] is None else product[low] + part
    for low in range(8):
        for strip in range(16):
            first = (strip * 8 + low) * 8
            store_halves(
                prod_scr, slice(first, first + 8), product[low][strip * 8 : strip * 8 + 8]
            )
    pieces = []
    for half in range(2):
        for w in range(8):
            for y in range(8):
                pieces.append(
                    load_halves(prod_scr, pl.ds((2 * y + half) * 64 + w, 8, stride=8))
                )
    source = x_ref[...].astype(F32)
    source = source.reshape(2, 8, 8, 8, 256).swapaxes(1, 2).reshape(tokens, 256)
    rows = (source + GELU_BACK * jnp.concatenate(pieces, axis=0)).astype(BF16).astype(F32)
    done = attend_rows(rows, gains_ref, entry_ref, leave_ref, offs_scr)
    done = done.reshape(2, 8, 8, 8, 256).swapaxes(1, 2).reshape(tokens, 256)
    out_ref[...] = done.astype(BF16)


def grid_kernel(
    x_ref,
    before_gains_ref,
    before_widen_ref,
    before_shrink_ref,
    gains_ref,
    entry_ref,
    leave_ref,
    offsets_ref,
    widen_ref,
    shrink_ref,
    out_ref,
    in_scr,
    back_scr,
    offs_scr,
):
    @pl.when(pl.program_id(0) == 0)
    def _():
        prepare_offsets(offsets_ref, offs_scr)

    count = x_ref.shape[1]
    tokens = count * 64
    came = x_ref[...].astype(F32).reshape(tokens, 256)
    came = feed_forward(came, before_gains_ref, before_widen_ref, before_shrink_ref)
    groups = count // 8
    came = came.astype(F32).reshape(64, groups, 8, 256).swapaxes(0, 1).reshape(tokens, 256)
    store_halves(in_scr, slice(0, tokens), came)
    places = [pl.ds((w // 8) * 512 + w % 8, 64, stride=8) for w in range(count)]
    rows = jnp.concatenate([load_halves(in_scr, place) for place in places], axis=0)
    attended = attend_rows(rows, gains_ref, entry_ref, leave_ref, offs_scr)
    done = feed_forward(attended, gains_ref, widen_ref, shrink_ref).astype(F32)
    for w, place in enumerate(places):
        store_halves(back_scr, place, done[w * 64 : (w + 1) * 64])
    done = load_halves(back_scr, slice(0, tokens)).reshape(groups, 64, 8, 256).swapaxes(0, 1)
    out_ref[...] = done.reshape(64, count, 256).astype(BF16)


def whole(shape):
    return pl.BlockSpec(shape, lambda i: (0,) * len(shape))


def conv_block(second_half, x, halo, left, right, weights):
    tokens, channels = STRIP * 64, x.shape[1]
    blocks = x.shape[0] // tokens
    steps = blocks // 2
    row = (64, channels)
    base = steps * second_half

    def above(i):
        return jnp.maximum(STRIP * (base + i) - 1, 0)

    def below(i):
        return jnp.minimum(STRIP * (base + i + 1), STRIP * blocks - 1)

    return pl.pallas_call(
        functools.partial(conv_block_kernel, second_half),
        grid=(steps,),
        in_specs=[
            pl.BlockSpec((tokens, channels), lambda i: (base + i, 0)),
            pl.BlockSpec(row, lambda i: (above(i), 0)),
            pl.BlockSpec(row, lambda i: (below(i), 0)),
        ]
        + [whole(halo.shape), whole(left.shape), whole(right.shape)]
        + [whole(w.shape) for w in weights],
        out_specs=pl.BlockSpec((tokens, channels), lambda i: (i, 0)),
        out_shape=jax.ShapeDtypeStruct((steps * tokens, channels), BF16),
        scratch_shapes=[
            pltpu.VMEM((2, (STRIP + 2) * 64, 128), F32),
            pltpu.VMEM((2, 48, channels), F32),
            pltpu.VMEM((2, tokens, 128), F32),
            pltpu.VMEM((64, 512), F32),
        ],
        compiler_params=pltpu.CompilerParams(vmem_limit_bytes=56 << 20),
        cost_estimate=pl.CostEstimate(
            flops=steps * tokens * 7000000,
            bytes_accessed=steps * tokens * 1024 + 4000000,
            transcendentals=0,
        ),
        name="conv_block",
    )(x, x, x, halo, left, right, *weights)


def grid_attend(x, weights):
    sources, count, channels = x.shape
    block = pl.BlockSpec((sources, GRID_WINDOWS, channels), lambda i: (0, i, 0))
    tokens = sources * GRID_WINDOWS
    return pl.pallas_call(
        grid_kernel,
        grid=(count // GRID_WINDOWS,),
        in_specs=[block] + [whole(w.shape) for w in weights],
        out_specs=block,
        out_shape=jax.ShapeDtypeStruct(x.shape, BF16),
        scratch_shapes=[
            pltpu.VMEM((2, tokens, 128), F32),
            pltpu.VMEM((2, tokens, 128), F32),
            pltpu.VMEM((64, 512), F32),
        ],
        compiler_params=pltpu.CompilerParams(vmem_limit_bytes=56 << 20),
        cost_estimate=pl.CostEstimate(
            flops=sources * count * 5000000,
            bytes_accessed=sources * count * 1024 + 4000000,
            transcendentals=0,
        ),
        name="grid_attend",
    )(x, *weights)


ROW = ("row_hi", "core")
GROUP = ("row_hi", "col")


def shards(
    radar_tiles,
    conv_scale,
    conv_shift,
    expand_weight,
    expand_bias,
    depth_kernel,
    depth_bias,
    project_weight,
    block_gains,
    block_entry,
    block_leave,
    block_offsets,
    block_widen,
    block_shrink,
    grid_gains,
    grid_entry,
    grid_leave,
    grid_offsets,
    grid_widen,
    grid_shrink,
):
    rows_here, cols_here, channels = radar_tiles.shape
    row_count, col_count = lax.axis_size(ROW), lax.axis_size("col")

    def shifted(values, axis, count, step):
        pairs = [(i, i + step) for i in range(count) if 0 <= i + step < count]
        return lax.ppermute(values, axis, pairs)

    x = radar_tiles.reshape(rows_here * cols_here, channels)
    even = lax.axis_index("core") == 0
    top, bottom = x[:cols_here], x[-cols_here:]
    near = lax.ppermute(jnp.where(even, bottom, top), "core", [(0, 1), (1, 0)])
    ends = [(r, r + 1) for r in range(1, row_count - 1, 2)]
    far = lax.ppermute(jnp.where(even, top, bottom), ROW, ends + [(b, a) for a, b in ends])
    above = jnp.where(even, far, near)
    below = jnp.where(even, near, far)
    edges = [
        jnp.concatenate([above[e][None], radar_tiles[:, e], below[e][None]], axis=0)
        for e in (-1, 0)
    ]
    left = shifted(edges[0], "col", col_count, 1)
    right = shifted(edges[1], "col", col_count, -1)
    weights = (
        conv_scale.reshape(1, -1),
        conv_shift.reshape(1, -1),
        expand_weight,
        expand_bias.reshape(1, -1),
        depth_kernel,
        depth_bias.reshape(1, -1),
        project_weight,
        block_gains,
        block_entry,
        block_leave,
        block_offsets,
    )
    grid_weights = (
        block_gains,
        block_widen,
        block_shrink,
        grid_gains,
        grid_entry,
        grid_leave,
        grid_offsets,
        grid_widen,
        grid_shrink,
    )
    group = row_count // 2 * col_count
    def spread(values):
        values = values.reshape(group, -1, channels)
        return lax.all_to_all(values, GROUP, split_axis=0, concat_axis=0, tiled=True)

    upper_there = spread(conv_block(False, x, above, left, right, weights))
    lower_there = spread(conv_block(True, x, below, left, right, weights))
    half = (rows_here // 2, cols_here, channels)
    upper = spread(grid_attend(upper_there, grid_weights)).reshape(half)
    lower = spread(grid_attend(lower_there, grid_weights)).reshape(half)
    result = jnp.pad(upper, ((0, half[0]), (0, 0), (0, 0)))
    result = lax.optimization_barrier(result)
    return lax.dynamic_update_slice(result, lower, (half[0], 0, 0))


def solution(mesh):
    inner = Mesh(mesh.devices.reshape(8, 2, 8), ("row_hi", "core", "col"))
    tiles = P(ROW, "col", None)
    return jax.shard_map(
        shards,
        mesh=inner,
        in_specs=(tiles,) + (P(),) * 19,
        out_specs=tiles,
        check_vma=False,
    )
```

```python
import functools
import math

import jax
import jax.numpy as jnp
from jax import lax
from jax.experimental import pallas as pl
from jax.experimental.pallas import tpu as pltpu
from jax.sharding import Mesh, PartitionSpec as P

WIN = 8
STRIP = 16
GRID_WINDOWS = 16
epsilon = 1e-05
F32 = jnp.float32
BF16 = jnp.bfloat16
GELU_A = math.sqrt(2.0 / math.pi)
GELU_B = GELU_A * 0.044715
LOG2E = math.log2(math.e)


GELU_S = GELU_B ** (1.0 / 3.0)
GELU_C = GELU_A / GELU_S
GELU_BACK = 0.5 / GELU_S


def scaled_gelu(z):
    return z + z * jnp.tanh(z * (z * z + GELU_C))


def dot(a, b):
    return jnp.dot(a, b, preferred_element_type=F32)


def load_halves(ref, where):
    return jnp.concatenate([ref[0, where, :], ref[1, where, :]], axis=-1)


def store_halves(ref, where, values):
    ref[0, where, :] = values[:, :128]
    ref[1, where, :] = values[:, 128:]


def layer_norm(values, gain):
    mean = jnp.mean(values, axis=-1, keepdims=True)
    center = values - mean
    spread = jnp.mean(center * center, axis=-1, keepdims=True)
    return (center * lax.rsqrt(spread + epsilon) * gain).astype(BF16)


def halves_dot(a, b):
    half = a.shape[0] // 2
    return jnp.concatenate([dot(a[:half], b), dot(a[half:], b)], axis=0)


def prepare_offsets(table_ref, offs_scr):
    heads = table_ref.shape[0]
    for pair in range(heads // 2):
        two = jnp.concatenate([table_ref[2 * pair], table_ref[2 * pair + 1]], axis=-1)
        offs_scr[:, pair * 128 : (pair + 1) * 128] = two * LOG2E


def attend_rows(rows, gains_ref, entry_ref, leave_ref, offs_scr):
    count, channels = rows.shape
    windows = count // 64
    normed = layer_norm(rows, gains_ref[0:1, :])
    scale = LOG2E / math.sqrt(32.0)
    qkv = [
        halves_dot(normed, entry_ref[:, part * channels : (part + 1) * channels])
        for part in range(3)
    ]
    queries = (qkv[0] * scale).astype(BF16)
    keys = qkv[1].astype(BF16)
    values = qkv[2].astype(BF16)
    lane = lax.broadcasted_iota(jnp.int32, (64, 128), 1) // 32
    masks = [(lane == h).astype(F32).astype(BF16) for h in range(4)]
    key_head = lax.broadcasted_iota(jnp.int32, (256, 256), 0) // 64
    out_head = lax.broadcasted_iota(jnp.int32, (256, 256), 1) // 64
    adder = (key_head == out_head).astype(F32).astype(BF16)
    sides = []
    for g in range(2):
        part = slice(g * 128, (g + 1) * 128)
        wide_part = slice(g * 256, (g + 1) * 256)
        probs = []
        for w in range(windows):
            here = slice(w * 64, (w + 1) * 64)
            wide = jnp.concatenate([keys[here, part] * m for m in masks], axis=0)
            score = lax.dot_general(
                queries[here, part], wide, (((1,), (1,)), ((), ())), preferred_element_type=F32
            )
            probs.append(jnp.exp2(score + offs_scr[:, wide_part]))
        prob = jnp.concatenate(probs, axis=0)
        prob = prob.astype(BF16)
        weight = prob / halves_dot(prob, adder).astype(BF16)
        mixed = []
        for w in range(windows):
            here = slice(w * 64, (w + 1) * 64)
            wide = jnp.concatenate([values[here, part] * m for m in masks], axis=0)
            mixed.append(dot(weight[here], wide).astype(BF16))
        sides.append(jnp.concatenate(mixed, axis=0))
    mixture = jnp.concatenate(sides, axis=-1)
    return (rows + halves_dot(mixture, leave_ref[...])).astype(BF16).astype(F32)


def feed_forward(attended, gains_ref, widen_ref, shrink_ref):
    second = layer_norm(attended, GELU_S * gains_ref[1:2, :])
    inner = widen_ref.shape[1]
    hidden = jnp.concatenate(
        [
            scaled_gelu(halves_dot(second, widen_ref[:, cut : cut + 256]).astype(BF16))
            for cut in range(0, inner, 256)
        ],
        axis=-1,
    )
    return (attended + GELU_BACK * halves_dot(hidden, shrink_ref[...])).astype(BF16)


def conv_block_kernel(second_half, x_ref, above_ref, below_ref, *refs):
    halo_ref, *refs = refs
    (
        left_ref,
        right_ref,
        scale_ref,
        shift_ref,
        expand_ref,
        expand_bias_ref,
        depth_ref,
        depth_bias_ref,
        project_ref,
        gains_ref,
        entry_ref,
        leave_ref,
        offsets_ref,
        out_ref,
        wide_scr,
        side_scr,
        prod_scr,
        offs_scr,
    ) = refs
    step = pl.program_id(0)
    steps = pl.num_programs(0)
    tokens = STRIP * 64
    inner = expand_ref.shape[1]

    @pl.when(step == 0)
    def _():
        prepare_offsets(offsets_ref, offs_scr)
        for which, ref in enumerate((left_ref, right_ref)):
            side = ref[...].astype(F32)
            for part in range(2):
                first = (2 * second_half + part) * STRIP
                side_scr[which, 24 * part : 24 * part + 18, :] = side[first : first + 18]

    above = above_ref[...].astype(F32)
    below = below_ref[...].astype(F32)
    halo = halo_ref[...].astype(F32)
    if second_half:
        below = jnp.where(step == steps - 1, halo, below)
    else:
        above = jnp.where(step == 0, halo, above)

    ext = STRIP + 2
    store_halves(wide_scr, slice(0, 64), above)
    store_halves(wide_scr, slice(64, 64 + tokens), x_ref[...].astype(F32))
    store_halves(wide_scr, slice(64 + tokens, 128 + tokens), below)
    where_in = lax.broadcasted_iota(jnp.int32, (ext, 8, 256), 1)
    scale = (GELU_S * scale_ref[...])[None]
    shift = (GELU_S * shift_ref[...])[None]

    def paired(cells):
        both = jnp.stack([cells[:10], cells[8:18]], axis=1)
        return (both * scale[None] + shift[None]).reshape(160, 256).astype(BF16)

    def side(which):
        rows = side_scr[which, pl.ds(pl.multiple_of(step * 24, 8), 24), :]
        return jnp.broadcast_to(rows[:ext, None, :], (ext, 8, 256))

    slots = [None] * 10
    for low in range(8):
        cells = load_halves(wide_scr, pl.ds(low, ext * 8, stride=8))
        slots[low + 1] = paired(cells.reshape(ext, 8, 256))
        if low == 7:
            rolled = pltpu.roll(cells, 1, 0).reshape(ext, 8, 256)
            slots[0] = paired(jnp.where(where_in == 0, side(0), rolled))
        if low == 0:
            rolled = pltpu.roll(cells, ext * 8 - 1, 0).reshape(ext, 8, 256)
            slots[9] = paired(jnp.where(where_in == 7, side(1), rolled))

    sub = lax.broadcasted_iota(jnp.int32, (16, 256), 0)

    def keep(condition, outside):
        value = jnp.where(outside, 0.0, 1.0)
        return jnp.where(condition, value, 1.0).astype(BF16)

    row, rows_of = lax.axis_index(ROW), lax.axis_size(ROW)
    col, cols_of = lax.axis_index("col"), lax.axis_size("col")
    if second_half:
        border = keep(sub >= 8, jnp.logical_and(step == steps - 1, row == rows_of - 1))
    else:
        border = keep(sub < 8, jnp.logical_and(step == 0, row == 0))
    at_left = keep(sub % 8 == 0, col == 0)
    at_right = keep(sub % 8 == 7, col == cols_of - 1)

    product = [None] * 8
    for cut in range(0, inner, 256):
        here = slice(cut, cut + 256)
        bias = (GELU_S * expand_bias_ref[:, here]).astype(BF16)
        cells = []
        for slot in range(10):
            one = scaled_gelu(dot(slots[slot], expand_ref[:, here]).astype(BF16) + bias)
            one = one.reshape(10, 16, 256)
            if second_half:
                one = jnp.concatenate([one[:9], one[9:] * border[None]], axis=0)
            else:
                one = jnp.concatenate([one[:1] * border[None], one[1:]], axis=0)
            if slot == 0:
                one = one * at_left[None]
            if slot == 9:
                one = one * at_right[None]
            cells.append(one)
        taps = [(GELU_S * GELU_BACK * depth_ref[k][:, here]).astype(BF16) for k in range(3)]
        depth_bias = (GELU_S * depth_bias_ref[:, here]).astype(BF16)
        for low in range(8):
            total = depth_bias[None]
            for s in range(3):
                for t in range(3):
                    tap = taps[s][t : t + 1][None]
                    total = total + cells[low + t][s : s + 8] * tap
            part = dot(scaled_gelu(total).reshape(128, 256), project_ref[here, :])
            product[low] = part if product[low] is None else product[low] + part
    for low in range(8):
        for strip in range(16):
            first = (strip * 8 + low) * 8
            store_halves(
                prod_scr, slice(first, first + 8), product[low][strip * 8 : strip * 8 + 8]
            )
    pieces = []
    for half in range(2):
        for w in range(8):
            for y in range(8):
                pieces.append(
                    load_halves(prod_scr, pl.ds((2 * y + half) * 64 + w, 8, stride=8))
                )
    source = x_ref[...].astype(F32)
    source = source.reshape(2, 8, 8, 8, 256).swapaxes(1, 2).reshape(tokens, 256)
    rows = (source + GELU_BACK * jnp.concatenate(pieces, axis=0)).astype(BF16).astype(F32)
    done = attend_rows(rows, gains_ref, entry_ref, leave_ref, offs_scr)
    done = done.reshape(2, 8, 8, 8, 256).swapaxes(1, 2).reshape(tokens, 256)
    out_ref[...] = done.astype(BF16)


def grid_kernel(
    x_ref,
    before_gains_ref,
    before_widen_ref,
    before_shrink_ref,
    gains_ref,
    entry_ref,
    leave_ref,
    offsets_ref,
    widen_ref,
    shrink_ref,
    out_ref,
    in_scr,
    back_scr,
    offs_scr,
):
    @pl.when(pl.program_id(0) == 0)
    def _():
        prepare_offsets(offsets_ref, offs_scr)

    count = x_ref.shape[1]
    tokens = count * 64
    came = x_ref[...].astype(F32).reshape(tokens, 256)
    came = feed_forward(came, before_gains_ref, before_widen_ref, before_shrink_ref)
    groups = count // 8
    came = came.astype(F32).reshape(64, groups, 8, 256).swapaxes(0, 1).reshape(tokens, 256)
    store_halves(in_scr, slice(0, tokens), came)
    places = [pl.ds((w // 8) * 512 + w % 8, 64, stride=8) for w in range(count)]
    rows = jnp.concatenate([load_halves(in_scr, place) for place in places], axis=0)
    attended = attend_rows(rows, gains_ref, entry_ref, leave_ref, offs_scr)
    done = feed_forward(attended, gains_ref, widen_ref, shrink_ref).astype(F32)
    for w, place in enumerate(places):
        store_halves(back_scr, place, done[w * 64 : (w + 1) * 64])
    done = load_halves(back_scr, slice(0, tokens)).reshape(groups, 64, 8, 256).swapaxes(0, 1)
    out_ref[...] = done.reshape(64, count, 256).astype(BF16)


def whole(shape):
    return pl.BlockSpec(shape, lambda i: (0,) * len(shape))


def conv_block(second_half, x, halo, left, right, weights):
    tokens, channels = STRIP * 64, x.shape[1]
    blocks = x.shape[0] // tokens
    steps = blocks // 2
    row = (64, channels)
    base = steps * second_half

    def above(i):
        return jnp.maximum(STRIP * (base + i) - 1, 0)

    def below(i):
        return jnp.minimum(STRIP * (base + i + 1), STRIP * blocks - 1)

    return pl.pallas_call(
        functools.partial(conv_block_kernel, second_half),
        grid=(steps,),
        in_specs=[
            pl.BlockSpec((tokens, channels), lambda i: (base + i, 0)),
            pl.BlockSpec(row, lambda i: (above(i), 0)),
            pl.BlockSpec(row, lambda i: (below(i), 0)),
        ]
        + [whole(halo.shape), whole(left.shape), whole(right.shape)]
        + [whole(w.shape) for w in weights],
        out_specs=pl.BlockSpec((tokens, channels), lambda i: (i, 0)),
        out_shape=jax.ShapeDtypeStruct((steps * tokens, channels), BF16),
        scratch_shapes=[
            pltpu.VMEM((2, (STRIP + 2) * 64, 128), F32),
            pltpu.VMEM((2, 48, channels), F32),
            pltpu.VMEM((2, tokens, 128), F32),
            pltpu.VMEM((64, 512), F32),
        ],
        compiler_params=pltpu.CompilerParams(vmem_limit_bytes=56 << 20),
        cost_estimate=pl.CostEstimate(
            flops=steps * tokens * 7000000,
            bytes_accessed=steps * tokens * 1024 + 4000000,
            transcendentals=0,
        ),
        name="conv_block",
    )(x, x, x, halo, left, right, *weights)


def grid_attend(x, weights):
    sources, count, channels = x.shape
    block = pl.BlockSpec((sources, GRID_WINDOWS, channels), lambda i: (0, i, 0))
    tokens = sources * GRID_WINDOWS
    return pl.pallas_call(
        grid_kernel,
        grid=(count // GRID_WINDOWS,),
        in_specs=[block] + [whole(w.shape) for w in weights],
        out_specs=block,
        out_shape=jax.ShapeDtypeStruct(x.shape, BF16),
        scratch_shapes=[
            pltpu.VMEM((2, tokens, 128), F32),
            pltpu.VMEM((2, tokens, 128), F32),
            pltpu.VMEM((64, 512), F32),
        ],
        compiler_params=pltpu.CompilerParams(vmem_limit_bytes=56 << 20),
        cost_estimate=pl.CostEstimate(
            flops=sources * count * 5000000,
            bytes_accessed=sources * count * 1024 + 4000000,
            transcendentals=0,
        ),
        name="grid_attend",
    )(x, *weights)


ROW = ("row_hi", "core")
GROUP = ("row_hi", "col")


def shards(
    radar_tiles,
    conv_scale,
    conv_shift,
    expand_weight,
    expand_bias,
    depth_kernel,
    depth_bias,
    project_weight,
    block_gains,
    block_entry,
    block_leave,
    block_offsets,
    block_widen,
    block_shrink,
    grid_gains,
    grid_entry,
    grid_leave,
    grid_offsets,
    grid_widen,
    grid_shrink,
):
    rows_here, cols_here, channels = radar_tiles.shape
    row_count, col_count = lax.axis_size(ROW), lax.axis_size("col")

    def shifted(values, axis, count, step):
        pairs = [(i, i + step) for i in range(count) if 0 <= i + step < count]
        return lax.ppermute(values, axis, pairs)

    x = radar_tiles.reshape(rows_here * cols_here, channels)
    even = lax.axis_index("core") == 0
    top, bottom = x[:cols_here], x[-cols_here:]
    near = lax.ppermute(jnp.where(even, bottom, top), "core", [(0, 1), (1, 0)])
    ends = [(r, r + 1) for r in range(1, row_count - 1, 2)]
    far = lax.ppermute(jnp.where(even, top, bottom), ROW, ends + [(b, a) for a, b in ends])
    above = jnp.where(even, far, near)
    below = jnp.where(even, near, far)
    edges = [
        jnp.concatenate([above[e][None], radar_tiles[:, e], below[e][None]], axis=0)
        for e in (-1, 0)
    ]
    left = shifted(edges[0], "col", col_count, 1)
    right = shifted(edges[1], "col", col_count, -1)
    weights = (
        conv_scale.reshape(1, -1),
        conv_shift.reshape(1, -1),
        expand_weight,
        expand_bias.reshape(1, -1),
        depth_kernel,
        depth_bias.reshape(1, -1),
        project_weight,
        block_gains,
        block_entry,
        block_leave,
        block_offsets,
    )
    grid_weights = (
        block_gains,
        block_widen,
        block_shrink,
        grid_gains,
        grid_entry,
        grid_leave,
        grid_offsets,
        grid_widen,
        grid_shrink,
    )
    group = row_count // 2 * col_count
    def spread(values):
        values = values.reshape(group, -1, channels)
        return lax.all_to_all(values, GROUP, split_axis=0, concat_axis=0, tiled=True)

    upper_there = spread(conv_block(False, x, above, left, right, weights))
    lower_there = spread(conv_block(True, x, below, left, right, weights))
    half = (rows_here // 2, cols_here, channels)
    upper = spread(grid_attend(upper_there, grid_weights)).reshape(half)
    lower = spread(grid_attend(lower_there, grid_weights)).reshape(half)
    result = jnp.pad(upper, ((0, half[0]), (0, 0), (0, 0)))
    result = lax.optimization_barrier(result)
    return lax.dynamic_update_slice(result, lower, (half[0], 0, 0))


def solution(mesh):
    inner = Mesh(mesh.devices.reshape(8, 2, 8), ("row_hi", "core", "col"))
    tiles = P(ROW, "col", None)
    return jax.shard_map(
        shards,
        mesh=inner,
        in_specs=(tiles,) + (P(),) * 19,
        out_specs=tiles,
        check_vma=False,
    )
```
